256 devices in a mesh: dom: 64 (over y, z, core), lvl: 4 (over x).
Axes of the slice: x: 4, y: 4, z: 8, core: 2. Of those that a mesh axis runs over, the one named last changes fastest.
Arguments:
- displacement: float32 [3, 1048576], P(None, ('dom', 'lvl')), may hold values from -1.8 to 1.8
- velocity: float32 [3, 1048576], P(None, ('dom', 'lvl')), may hold values from -6 to 6
- inverse_mass: float32 [1048576], P(('dom', 'lvl')), may hold values from 0.5 to 2
- levels: int32 [16384], P(('dom', 'lvl')), may hold values from 0 to 3, as said below
- first_lame: float32 [16384], P(('dom', 'lvl')), may hold values from 0.125 to 32
- shear_modulus: float32 [16384], P(('dom', 'lvl')), may hold values from 0.125 to 32
- connectivity: int32 [125, 16384], P(None, ('dom', 'lvl')), may hold values from 0 to 4607, as said below
- owner_list: int32 [131072], P(('dom', 'lvl')), may hold values from 0 to 4095, as said below
Outputs:
- new_displacement: float32 [3, 1048576], P(None, ('dom', 'lvl'))
- new_velocity: float32 [3, 1048576], P(None, ('dom', 'lvl'))
The draws below stay inside these ranges and needn't reach their ends.
Inputs may be any that keep to these rules, and one draw needn't show every extreme that they name: `levels`: levels 0 to 3. On each device at most 16 elements have level 3, at most 24 level 2 or more, at most 32 level 1 or more; each of these bounds is met on one device of every row of 4 consecutive devices that share a dom index, and every such row holds exactly 32 elements of level 3. `connectivity`: the 125 entries of an element are distinct and form a conforming hexahedral mesh of slabs 2 elements thick chained from device to device in a loop; entries at least 4096 are ghost slots of the next device. `owner_list`: on each device, distinct owned nodes, matching the ghost slots of the previous device.
All inputs are finite; a program needn't handle non-finite values.
Results may differ from the reference program's by a relative error of at most 0.0001.
Values sent between devices are 32-bit elements; how exact they have to be, the bound alone decides.
No kernel may reach another device: no remote copies, remote signals or barrier semaphores. Data moves between devices by JAX's collectives and lax.ppermute only.
A program may use at most 64 MiB of HBM per device.

```python
import math
import jax
import jax.numpy as jnp
import numpy as np
from jax import lax

SLAB_X = 2
SLAB_Y = 4
SLAB_Z = 8
ELEMS_DEV = 64
NODES_DEV = 4096
GHOSTS_DEV = 512
FINE_MOST = 16
MID_MOST = 24
COARSE_MOST = 32
ELEMS = 16384
NODES = 1048576
N_LVL = 4
DEVICES = 256


def mesh_tables(key):
    base = jax.random.fold_in(key, 7)
    width_y = 4 * SLAB_Y
    width_z = 4 * SLAB_Z
    plane = width_y * width_z

    def device_perms(device):
        device_key = jax.random.fold_in(base, device)
        node_perm = jax.random.permutation(jax.random.fold_in(device_key, 1), NODES_DEV).astype(jnp.int32)
        ghost_perm = jax.random.permutation(jax.random.fold_in(device_key, 2), GHOSTS_DEV).astype(jnp.int32)
        return (node_perm, ghost_perm)
    node_perms, ghost_perms = jax.vmap(device_perms)(jnp.arange(DEVICES, dtype=jnp.int32))
    local_point = jnp.arange(125, dtype=jnp.int32)
    point_x = local_point // 25
    point_y = local_point // 5 % 5
    point_z = local_point % 5
    element = jnp.arange(ELEMS_DEV, dtype=jnp.int32)
    elem_x = element // (SLAB_Y * SLAB_Z)
    elem_y = element // SLAB_Z % SLAB_Y
    elem_z = element % SLAB_Z
    grid_x = 4 * elem_x[None, :] + point_x[:, None]
    grid_y = (4 * elem_y[None, :] + point_y[:, None]) % width_y
    grid_z = (4 * elem_z[None, :] + point_z[:, None]) % width_z
    plane_index = grid_y * width_z + grid_z
    own_index = jnp.clip(grid_x * plane + plane_index, 0, NODES_DEV - 1)

    def device_connect(node_perm, ghost_perm):
        return jnp.where(grid_x < 4 * SLAB_X, node_perm[own_index], NODES_DEV + ghost_perm[plane_index]).astype(jnp.int32)
    connect_all = jax.vmap(device_connect)(node_perms, ghost_perms)
    connect_all = jnp.transpose(connect_all, (1, 0, 2)).reshape(125, DEVICES * ELEMS_DEV)
    previous_ghost = jnp.roll(ghost_perms, 1, axis=0)

    def device_owner(node_perm, ghost_perm):
        inverse = jnp.zeros((GHOSTS_DEV,), jnp.int32).at[ghost_perm].set(jnp.arange(GHOSTS_DEV, dtype=jnp.int32))
        return node_perm[inverse]
    owner_all = jax.vmap(device_owner)(node_perms, previous_ghost).reshape(DEVICES * GHOSTS_DEV)
    return (connect_all, owner_all)


def draw_connectivity(key, part):
    return mesh_tables(key)[0]


def draw_owner_list(key, part):
    return mesh_tables(key)[1]


def draw_levels(key, part):
    row_count = DEVICES // N_LVL
    slots = jnp.arange(N_LVL, dtype=jnp.int32)

    def one_row(row):
        row_key = jax.random.fold_in(key, row)
        top = jax.random.randint(jax.random.fold_in(row_key, 1), (), 0, N_LVL)
        cuts = jnp.sort(jax.random.randint(jax.random.fold_in(row_key, 2), (N_LVL - 2,), 0, FINE_MOST + 1))
        bounds = jnp.concatenate([jnp.zeros((1,), jnp.int32), cuts.astype(jnp.int32), jnp.full((1,), FINE_MOST, jnp.int32)])
        pieces = bounds[1:] - bounds[:-1]
        other = jnp.clip(slots - (slots > top).astype(jnp.int32), 0, N_LVL - 2)
        fine_counts = jnp.where(slots == top, FINE_MOST, pieces[other])
        extra_mid = jax.random.randint(jax.random.fold_in(row_key, 3), (N_LVL,), 0, MID_MOST - FINE_MOST + 1)
        extra_mid = jnp.where(slots == top, MID_MOST - FINE_MOST, extra_mid)
        extra_coarse = jax.random.randint(jax.random.fold_in(row_key, 4), (N_LVL,), 0, COARSE_MOST - MID_MOST + 1)
        extra_coarse = jnp.where(slots == top, COARSE_MOST - MID_MOST, extra_coarse)
        mid_counts = fine_counts + extra_mid
        coarse_counts = mid_counts + extra_coarse

        def one_device(slot):
            order = jax.random.permutation(jax.random.fold_in(row_key, 10 + slot), ELEMS_DEV).astype(jnp.int32)
            level_of = (order < fine_counts[slot]).astype(jnp.int32) + (order < mid_counts[slot]).astype(jnp.int32) + (order < coarse_counts[slot]).astype(jnp.int32)
            return level_of
        return jax.vmap(one_device)(slots)
    return jax.vmap(one_row)(jnp.arange(row_count, dtype=jnp.int32)).reshape(DEVICES * ELEMS_DEV).astype(jnp.int32)


def level_factor(key, part):
    level_of = draw_levels(key, part)
    return jnp.where(level_of == 0, 0.25, jnp.where(level_of == 1, 1.0, jnp.where(level_of == 2, 4.0, 16.0))).astype(jnp.float32)


def material_unit(key, salt):
    material_key = jax.random.fold_in(jax.random.fold_in(key, 90001), salt)
    return jax.random.uniform(material_key, (ELEMS,), jnp.float32, 0.0, 1.0)


def draw_first_lame(key, part):
    unit = material_unit(key, 1)
    base_value = 0.5 * jnp.exp(unit * jnp.log(4.0))
    return (base_value * level_factor(key, part)).astype(jnp.float32)


def draw_shear_modulus(key, part):
    unit = material_unit(key, 2)
    base_value = 0.5 * jnp.exp(unit * jnp.log(4.0))
    return (base_value * level_factor(key, part)).astype(jnp.float32)


def block_levels(rng, extent, cuts, least, high):
    def one(axis_at, shards_of):
        steps = jax.random.uniform(jax.random.fold_in(jax.random.fold_in(rng, 6), axis_at), (shards_of,), jnp.float32, least / len(cuts), high / len(cuts))
        return jnp.repeat(jnp.exp(steps), extent[axis_at] // shards_of).reshape((-1,) + (1,) * (len(extent) - axis_at - 1))

    factor_of = one(*cuts[0])
    for cut in cuts[1:]:
        factor_of = factor_of * one(*cut)
    return factor_of


def gaussian(key, shape, spread, bound, cuts=(), kind=jnp.bfloat16):
    values = spread * jax.random.normal(key, shape, jnp.float32)
    if cuts:
        values = values * block_levels(key, shape, cuts, -0.22, 0.18)
    return jnp.clip(values, -bound, bound).astype(kind)


def setup_inputs(seed: int = 0) -> dict:
    key_list = jax.random.split(jax.random.key(seed), 9)
    return {
        "displacement": gaussian(key_list[0], (3, NODES), 0.3, 1.8, ((1, 256),), jnp.float32),
        "velocity": gaussian(key_list[1], (3, NODES), 1.0, 6.0, ((1, 256),), jnp.float32),
        "inverse_mass": jnp.clip(jnp.exp(math.log(2.0) - 1.3862944 * jax.random.uniform(key_list[2], (NODES,), jnp.float32) ** block_levels(key_list[2], (NODES,), ((0, 256),), -0.2, 0.2)), 0.5, 2.0),
        "levels": draw_levels(jax.random.fold_in(key_list[8], 71), 0),
        "first_lame": draw_first_lame(jax.random.fold_in(key_list[8], 71), 0),
        "shear_modulus": draw_shear_modulus(jax.random.fold_in(key_list[8], 71), 0),
        "connectivity": draw_connectivity(jax.random.fold_in(key_list[8], 71), 0),
        "owner_list": draw_owner_list(jax.random.fold_in(key_list[8], 71), 0),
    }


substep_length = 0.01

def lobatto_tables():
    points = np.array([-1.0, -np.sqrt(3.0 / 7.0), 0.0, np.sqrt(3.0 / 7.0), 1.0])
    weights = np.array([0.1, 49.0 / 90.0, 32.0 / 45.0, 49.0 / 90.0, 0.1])
    factor = np.array([np.prod([points[i] - points[k] for k in range(5) if k != i]) for i in range(5)])
    matrix = np.zeros((5, 5))
    for i in range(5):
        for j in range(5):
            if i == j:
                matrix[i, j] = sum((1.0 / (points[i] - points[k]) for k in range(5) if k != i))
            else:
                matrix[i, j] = factor[i] / (factor[j] * (points[i] - points[j]))
    cube = weights[:, None, None] * weights[None, :, None] * weights[None, None, :]
    return (jnp.asarray(matrix, jnp.float32), jnp.asarray(cube, jnp.float32))

def element_force(values, lame_first, lame_shear, tables):
    derivative, weight_cube = tables
    highest = lax.Precision.HIGHEST
    field = values.reshape(3, 5, 5, 5, -1)
    along_first = jnp.einsum('pi,cijkb->cpjkb', derivative, field, precision=highest)
    along_second = jnp.einsum('qj,cijkb->ciqkb', derivative, field, precision=highest)
    along_third = jnp.einsum('rk,cijkb->cijrb', derivative, field, precision=highest)
    gradient = jnp.stack([along_first, along_second, along_third], axis=1)
    divergence = along_first[0] + along_second[1] + along_third[2]
    unit_matrix = jnp.eye(3, dtype=jnp.float32)
    stress = lame_shear * (gradient + jnp.swapaxes(gradient, 0, 1)) + lame_first * divergence[None, None] * unit_matrix[:, :, None, None, None, None]
    weighted = stress * weight_cube[None, None, :, :, :, None]
    forces = jnp.einsum('pi,cpjkb->cijkb', derivative, weighted[:, 0], precision=highest)
    forces = forces + jnp.einsum('qj,ciqkb->cijkb', derivative, weighted[:, 1], precision=highest)
    forces = forces + jnp.einsum('rk,cijrb->cijkb', derivative, weighted[:, 2], precision=highest)
    return forces.reshape(3, 125, -1)

def reference(displacement, velocity, inverse_mass, levels, first_lame, shear_modulus, connectivity, owner_list):
    tables = lobatto_tables()
    local_ids = connectivity.reshape(125, DEVICES, ELEMS_DEV)
    device_ids = jnp.arange(DEVICES, dtype=jnp.int32)[None, :, None]
    successor = (device_ids + 1) % DEVICES
    owner_table = owner_list.reshape(DEVICES, GHOSTS_DEV)
    ghost_slot = jnp.clip(local_ids - NODES_DEV, 0, GHOSTS_DEV - 1)
    ghost_node = owner_table[successor, ghost_slot]
    global_ids = jnp.where(local_ids < NODES_DEV, device_ids * NODES_DEV + local_ids, successor * NODES_DEV + ghost_node).astype(jnp.int32)
    global_blocks = jnp.transpose(global_ids, (1, 0, 2))
    period = jnp.where(levels == 0, 8, jnp.where(levels == 1, 4, jnp.where(levels == 2, 2, 1))).astype(jnp.int32)
    lame_blocks = first_lame.reshape(DEVICES, ELEMS_DEV)
    shear_blocks = shear_modulus.reshape(DEVICES, ELEMS_DEV)
    for substep in range(8):
        weight = jnp.where(substep % period == 0, period.astype(jnp.float32), jnp.float32(0.0)).reshape(DEVICES, ELEMS_DEV)
        current = displacement

        def add_block(total, block_item):
            nodes_of, lame_first, lame_shear, weight_row = block_item
            forces = element_force(current[:, nodes_of], lame_first, lame_shear, tables) * weight_row[None, None, :]
            return (total.at[:, nodes_of].add(forces), None)
        assembled = lax.scan(add_block, jnp.zeros((3, NODES), jnp.float32), (global_blocks, lame_blocks, shear_blocks, weight))[0]
        velocity = velocity - substep_length * inverse_mass[None, :] * assembled
        displacement = displacement + substep_length * velocity
    return (displacement, velocity)
```

```python
import jax
import jax.numpy as jnp
import numpy as np
from jax import lax
from jax.experimental import pallas as pl
from jax.experimental.pallas import tpu as pltpu
from jax.sharding import PartitionSpec as P

substep_length = 0.01
AXES = ("dom", "lvl")
SUB, LANE = 8, 128
VALUES = 7
POINTS = 64
ROWS = VALUES * 32 + 16
STAGE = VALUES * POINTS + 16
F32 = jnp.float32


def lobatto():
    points = np.array([-1.0, -np.sqrt(3.0 / 7.0), 0.0, np.sqrt(3.0 / 7.0), 1.0])
    weights = np.array([0.1, 49.0 / 90.0, 32.0 / 45.0, 49.0 / 90.0, 0.1])
    factor = np.array(
        [np.prod([points[i] - points[k] for k in range(5) if k != i]) for i in range(5)]
    )
    matrix = np.zeros((5, 5))
    for i in range(5):
        for j in range(5):
            if i == j:
                matrix[i, j] = sum((1.0 / (points[i] - points[k]) for k in range(5) if k != i))
            else:
                matrix[i, j] = factor[i] / (factor[j] * (points[i] - points[j]))
    return matrix, weights


DER, WEI = lobatto()


def line_derivative(u):
    s0, s1 = u[0] + u[4], u[1] + u[3]
    o0, o1 = u[4] - u[0], u[3] - u[1]
    two = u[2] + u[2]
    e0, e1 = s0 - two, s1 - two
    out = [None] * 5
    for p in range(2):
        even = float((DER[p, 0] + DER[p, 4]) / 2) * e0 + float((DER[p, 1] + DER[p, 3]) / 2) * e1
        odd = float((DER[p, 4] - DER[p, 0]) / 2) * o0 + float((DER[p, 3] - DER[p, 1]) / 2) * o1
        out[p] = odd + even
        out[4 - p] = odd - even
    out[2] = float(DER[2, 4]) * o0 + float(DER[2, 3]) * o1
    return out


def line_transposed(s):
    p0, p1 = s[0] + s[4], s[1] + s[3]
    m0, m1 = s[4] - s[0], s[3] - s[1]
    out = [None] * 5
    for i in range(2):
        minus = float((DER[4, i] - DER[0, i]) / 2) * m0 + float((DER[3, i] - DER[1, i]) / 2) * m1
        plus = (
            float((DER[0, i] + DER[4, i]) / 2) * p0
            + float((DER[1, i] + DER[3, i]) / 2) * p1
            + float(DER[2, i]) * s[2]
        )
        out[i] = minus + plus
        out[4 - i] = minus - plus
    out[2] = float(DER[4, 2]) * m0 + float(DER[3, 2]) * m1
    return out


def lanes(x, index):
    return jnp.take_along_axis(x, index, axis=1, mode="promise_in_bounds")


def as_column(row):
    n = row.shape[1]
    diag = lax.broadcasted_iota(jnp.int32, (n, n), 0) == lax.broadcasted_iota(jnp.int32, (n, n), 1)
    return jnp.sum(jnp.where(diag, jnp.broadcast_to(row, (n, n)), 0.0), axis=1, keepdims=True)


def pack_kernel(u, v, m, lev, lam, mu, conn, own, out, index, stage):
    for i in range(16):
        r = 25 * (i // 4) + 5 * (i % 4)
        stage[4 * i : 4 * i + 4, :] = conn[r : r + 4, :]
    packed = jnp.concatenate([stage[0:32, :], stage[32:64, :]], axis=1)
    index[...] = packed
    for t in range(4):
        part = index[8 * t : 8 * t + 8, :]
        high, low = part >> 7, part & 127
        acc = [jnp.zeros((SUB, LANE), F32) for _ in range(VALUES)]
        for r in range(32):
            here = high == r
            for k in range(VALUES):
                if k < 3:
                    row = u[k : k + 1, r * LANE : (r + 1) * LANE]
                elif k < 6:
                    row = v[k - 3 : k - 2, r * LANE : (r + 1) * LANE]
                else:
                    row = m[r : r + 1, :]
                got = lanes(jnp.broadcast_to(row, (SUB, LANE)), low)
                acc[k] = jnp.where(here, got, acc[k])
        for k in range(VALUES):
            out[k * 32 + 8 * t : k * 32 + 8 * t + 8, :] = acc[k]
    out[VALUES * 32 : ROWS, :] = jnp.zeros((16, LANE), F32)
    corner = {n: conn[r : r + 1, :].astype(F32) for n, r in (("o", 0), ("z", 4), ("y", 20), ("x", 100))}
    column = {n: as_column(c) for n, c in corner.items()}
    n = 64
    which = lax.broadcasted_iota(jnp.int32, (n, n), 0).astype(F32)

    def match(col, row):
        hit = column[col] == corner[row]
        return jnp.sum(jnp.where(hit, which + 1.0, 0.0), axis=0, keepdims=True) - 1.0

    slot = jnp.zeros((n, 1), F32)
    for j in range(4):
        number = (lax.broadcasted_iota(jnp.int32, (n, LANE), 1) + (j * LANE + 1)).astype(F32)
        hit = column["o"] == own[j : j + 1, :].astype(F32)
        slot = slot + jnp.sum(jnp.where(hit, number, 0.0), axis=1, keepdims=True)
    diag = lax.broadcasted_iota(jnp.int32, (n, n), 0) == lax.broadcasted_iota(jnp.int32, (n, n), 1)
    slot_row = jnp.sum(jnp.where(diag, slot, 0.0), axis=0, keepdims=True)
    level = lev[...]
    rows = [
        lam[...],
        mu[...],
        jnp.where(level == 0, 8, jnp.where(level == 1, 4, jnp.where(level == 2, 2, 1))).astype(F32),
        match("o", "z"),
        match("z", "o"),
        match("o", "y"),
        match("y", "o"),
        match("o", "x"),
        match("x", "o"),
        jnp.where(corner["x"] >= 4096.0, corner["x"] - 4096.0, -1.0),
        jnp.where(slot_row > 0.5, slot_row - 1.0, -2.0),
    ]
    for i, row in enumerate(rows):
        out[VALUES * 32 + i : VALUES * 32 + i + 1, 0:64] = row


def place_kernel(index, place):
    acc = jnp.zeros((64, LANE), F32)
    lane = lax.broadcasted_iota(jnp.int32, (32, LANE), 1).astype(F32)
    sub = lax.broadcasted_iota(jnp.int32, (32, LANE), 0)
    wide = lax.broadcasted_iota(jnp.int32, (LANE, LANE), 0)
    for r in range(32):
        row = index[r : r + 1, :]
        here = sub == (row >> 7)
        left = jnp.concatenate(
            [jnp.where(here, float(r), 0.0), jnp.where(here, lane, 0.0)], axis=0
        ).astype(jnp.bfloat16)
        right = jnp.where(wide == (row & 127), 1.0, 0.0).astype(jnp.bfloat16)
        acc = acc + lax.dot_general(
            left, right, (((1,), (1,)), ((), ())), preferred_element_type=F32
        )
    place[...] = acc.astype(jnp.int32)


def pt(c, a, b, k):
    return ((c * 5 + a) * 5 + b) * 5 + k


def main_kernel(
    flags, own, even, odd, r1, r2, r3, s1, s2, s3, place, new_u, new_v,
    stage, disp, gy, gz, force, tab, table,
):
    def at(ref, row):
        if isinstance(row, int):
            return ref[row * SUB : row * SUB + SUB, :]
        return ref[pl.ds(pl.multiple_of(row * SUB, SUB), SUB), :]

    def put(ref, row, value):
        if isinstance(row, int):
            ref[row * SUB : row * SUB + SUB, :] = value
        else:
            ref[pl.ds(pl.multiple_of(row * SUB, SUB), SUB), :] = value

    parity, me = flags[0], flags[1]
    lane = lax.broadcasted_iota(jnp.int32, (SUB, LANE), 1)
    sub = lax.broadcasted_iota(jnp.int32, (SUB, LANE), 0)
    right_half = lane >= 64
    is_odd = jnp.full((SUB, LANE), parity, jnp.int32) == 1
    base = VALUES * POINTS

    def spread(get, position):
        for r in range(0, VALUES * 32, SUB):
            x = get(r)
            k, q = r // 32, r % 32
            stage[pl.ds((k * POINTS + q) * SUB + position, SUB, stride=SUB), :] = x
            stage[pl.ds((k * POINTS + q + 32) * SUB + position, SUB, stride=SUB), :] = pltpu.roll(x, 64, 1)
        for r in range(0, 16, SUB):
            stage[pl.ds((base + r) * SUB + position, SUB, stride=SUB), :] = get(VALUES * 32 + r)

    spread(lambda r: own[r : r + SUB, :], 4)
    spread(lambda r: jnp.where(is_odd, even[r : r + SUB, :], odd[r : r + SUB, :]), 0)
    for other, near, cross in ((1, r1, s1), (2, r2, s2), (3, r3, s3)):
        partner = lax.bitwise_xor(me, other)
        away = partner - me
        spread(lambda r, near=near: near[r : r + SUB, :], 4 + away)
        spread(lambda r, cross=cross: cross[r : r + SUB, :], jnp.where(away > 0, away, away + 8))
    last = sub == 7
    for r in range(0, ROWS, SUB):
        x = jnp.where(is_odd, odd[r : r + SUB, :], even[r : r + SUB, :])
        y = pltpu.roll(x, 64, 1)
        if r < VALUES * 32:
            k, q = r // 32, r % 32
            pairs = ((k * POINTS + q, y), (k * POINTS + q + 32, x))
        else:
            pairs = ((base + r - VALUES * 32, y),)
        for row, value in pairs:
            where = pl.ds(row * SUB + 7, SUB, stride=SUB)
            stage[where, :] = jnp.where(right_half, value, stage[where, :])

    elem = [at(stage, base + i) for i in range(11)]
    lame, shear = elem[0], elem[1]
    period = elem[2].astype(jnp.int32)
    half = jnp.where(right_half, 64, 0)
    next_z = jnp.maximum(elem[3], 0.0).astype(jnp.int32) + half
    prev_z = jnp.maximum(elem[4], 0.0).astype(jnp.int32) + half
    next_y = jnp.maximum(elem[5], 0.0).astype(jnp.int32) + half
    prev_y = jnp.maximum(elem[6], 0.0).astype(jnp.int32) + half
    ghost = elem[9]
    corner = elem[10]
    corner_next = jnp.where(last, pltpu.roll(corner, 64, 1), pltpu.roll(corner, 7, 0))
    ghost_t, corner_t = ghost.T, corner_next.T
    number = lax.broadcasted_iota(jnp.int32, (64, LANE), 0).astype(F32)
    to_next = jnp.zeros((SUB, LANE), F32)
    to_prev = jnp.zeros((SUB, LANE), F32)
    for s in range(SUB):
        hit = corner_t[0:64, s : s + 1] == ghost[s : s + 1, :]
        found = jnp.sum(jnp.where(hit, number, 0.0), axis=0, keepdims=True)
        to_next = jnp.where(sub == s, found, to_next)
        hit = ghost_t[0:64, s : s + 1] == corner_next[s : s + 1, :]
        found = jnp.sum(jnp.where(hit, number, 0.0), axis=0, keepdims=True)
        to_prev = jnp.where(sub == s, found, to_prev)
    to_next = to_next.astype(jnp.int32)
    to_prev = to_prev.astype(jnp.int32)
    inner = elem[7] >= 0.0
    tail = last & right_half
    next_x = jnp.where(
        inner, elem[7].astype(jnp.int32) + half, jnp.where(tail, lane, jnp.where(last, to_next + 64, to_next))
    )
    next_cross = jnp.logical_not(inner | last)
    inner = elem[8] >= 0.0
    from_prev = jnp.where(tail, pltpu.roll(to_prev, 64, 1), pltpu.roll(to_prev, 1, 0))
    prev_x = jnp.where(inner, elem[8].astype(jnp.int32) + half, from_prev)
    prev_cross = jnp.logical_not(inner | tail)
    no_prev = (sub == 0) & jnp.logical_not(inner)
    step = jnp.float32(substep_length)

    for c in range(3):
        for p in range(POINTS):
            a, b, k = p // 16, p // 4 % 4, p % 4
            put(disp, pt(c, a, b, k), at(stage, c * POINTS + p))
    for p in range(POINTS):
        put(stage, 6 * POINTS + p, step * at(stage, 6 * POINTS + p))

    def one_substep(s, carry):
        weight = jnp.where((s & (period - 1)) == 0, period, 0).astype(F32)
        lame_s, shear_s = lame * weight, shear * weight
        for b in range(5):
            for k in range(5):
                w = float(WEI[b] * WEI[k])
                put(tab, b * 5 + k, lame_s * w)
                put(tab, 25 + b * 5 + k, shear_s * w)

        def expand(c, carry):
            o = c * 125
            for a in range(4):
                for b in range(4):
                    put(disp, o + pt(0, a, b, 4), lanes(at(disp, o + pt(0, a, b, 0)), next_z))
            for a in range(4):
                for k in range(5):
                    put(disp, o + pt(0, a, 4, k), lanes(at(disp, o + pt(0, a, 0, k)), next_y))
            for b in range(5):
                for k in range(5):
                    x = at(disp, o + pt(0, 0, b, k))
                    value = jnp.where(next_cross, lanes(pltpu.roll(x, 7, 0), next_x), lanes(x, next_x))
                    put(disp, o + pt(0, 4, b, k), value)
            return carry

        lax.fori_loop(0, 3, expand, 0)

        def planes(j, carry):
            o = j * 25
            plane = [[at(disp, o + b * 5 + k) for k in range(5)] for b in range(5)]
            for b in range(5):
                for k, value in enumerate(line_derivative(plane[b])):
                    put(gz, o + b * 5 + k, value)
            for k in range(5):
                for b, value in enumerate(line_derivative([plane[b][k] for b in range(5)])):
                    put(gy, o + b * 5 + k, value)
            return carry

        lax.fori_loop(0, 15, planes, 0)

        def stresses(b, carry):
            for k in range(5):
                gx = [
                    line_derivative([at(disp, b * 5 + pt(c, a, 0, k)) for a in range(5)])
                    for c in range(3)
                ]
                lw, mw = at(tab, b * 5 + k), at(tab, 25 + b * 5 + k)
                scaled = [(float(WEI[a]) * lw, float(WEI[a]) * mw) for a in range(3)]
                scaled = [(x, y, y + y) for x, y in scaled]
                sx = [[None] * 5 for _ in range(3)]
                for a in range(5):
                    la, ma, m2 = scaled[min(a, 4 - a)]
                    rows = [b * 5 + pt(c, a, 0, k) for c in range(3)]
                    y = [at(gy, r) for r in rows]
                    z = [at(gz, r) for r in rows]
                    xx, yx, zx = gx[0][a], gx[1][a], gx[2][a]
                    spread_of = la * (xx + y[1] + z[2])
                    sx[0][a] = m2 * xx + spread_of
                    sx[1][a] = ma * (yx + y[0])
                    sx[2][a] = ma * (zx + z[0])
                    yz = ma * (y[2] + z[1])
                    put(gy, rows[0], sx[1][a])
                    put(gy, rows[1], m2 * y[1] + spread_of)
                    put(gy, rows[2], yz)
                    put(gz, rows[0], sx[2][a])
                    put(gz, rows[1], yz)
                    put(gz, rows[2], m2 * z[2] + spread_of)
                for c in range(3):
                    for a, value in enumerate(line_transposed(sx[c])):
                        put(force, b * 5 + pt(c, a, 0, k), value)
            return carry

        lax.fori_loop(0, 5, stresses, 0)

        def gather_planes(j, carry):
            o = j * 25
            total = [[at(force, o + b * 5 + k) for k in range(5)] for b in range(5)]
            for b in range(5):
                for k, value in enumerate(line_transposed([at(gz, o + b * 5 + k) for k in range(5)])):
                    total[b][k] = total[b][k] + value
            for k in range(5):
                for b, value in enumerate(line_transposed([at(gy, o + b * 5 + k) for b in range(5)])):
                    total[b][k] = total[b][k] + value
            for b in range(5):
                for k in range(5):
                    put(force, o + b * 5 + k, total[b][k])
            return carry

        lax.fori_loop(0, 15, gather_planes, 0)

        def fold(c, carry):
            o = c * 125
            for b in range(5):
                for k in range(5):
                    x = at(force, o + pt(0, 4, b, k))
                    value = jnp.where(prev_cross, lanes(pltpu.roll(x, 1, 0), prev_x), lanes(x, prev_x))
                    row = o + pt(0, 0, b, k)
                    put(force, row, at(force, row) + jnp.where(no_prev, 0.0, value))
            for a in range(4):
                for k in range(5):
                    row = o + pt(0, a, 0, k)
                    put(force, row, at(force, row) + lanes(at(force, o + pt(0, a, 4, k)), prev_y))
            for p in range(POINTS):
                a, b, k = p // 16, p // 4 % 4, p % 4
                row = o + pt(0, a, b, k)
                f = at(force, row)
                if k == 0:
                    f = f + lanes(at(force, o + pt(0, a, b, 4)), prev_z)
                vrow = (3 + c) * POINTS + p
                vel = at(stage, vrow) - at(stage, 6 * POINTS + p) * f
                put(stage, vrow, vel)
                put(disp, row, at(disp, row) + step * vel)
            return carry

        lax.fori_loop(0, 3, fold, 0)
        return carry

    lax.fori_loop(0, 8, one_substep, 0)

    left4 = lax.broadcasted_iota(jnp.int32, (4, LANE), 1) < 64
    for c in range(3):
        for q in range(0, 32, 4):
            a, b = q // 16, q // 4 % 4
            x = disp[pl.ds(pt(c, a, b, 0) * SUB + 4, 4, stride=SUB), :]
            y = disp[pl.ds(pt(c, a + 2, b, 0) * SUB + 4, 4, stride=SUB), :]
            table[c * 32 + q : c * 32 + q + 4, :] = jnp.where(left4, x, pltpu.roll(y, 64, 1))
        for q in range(0, 32, SUB):
            x = stage[pl.ds(((3 + c) * POINTS + q) * SUB + 4, SUB, stride=SUB), :]
            y = stage[pl.ds(((3 + c) * POINTS + q + 32) * SUB + 4, SUB, stride=SUB), :]
            table[(3 + c) * 32 + q : (3 + c) * 32 + q + SUB, :] = jnp.where(
                right_half, pltpu.roll(y, 64, 1), x
            )
    for t in range(4):
        high, low = place[8 * t : 8 * t + 8, :], place[32 + 8 * t : 32 + 8 * t + 8, :]
        acc = [jnp.zeros((SUB, LANE), F32) for _ in range(6)]
        for q in range(32):
            here = high == q
            for k in range(6):
                row = table[k * 32 + q : k * 32 + q + 1, :]
                acc[k] = jnp.where(here, lanes(jnp.broadcast_to(row, (SUB, LANE)), low), acc[k])
        for k in range(6):
            for j in range(SUB):
                n = (8 * t + j) * LANE
                ref = new_u if k < 3 else new_v
                ref[k % 3 : k % 3 + 1, n : n + LANE] = acc[k][j : j + 1, :]


VMEM = pl.BlockSpec(memory_space=pltpu.VMEM)
SMEM = pl.BlockSpec(memory_space=pltpu.SMEM)


def per_device(displacement, velocity, inverse_mass, levels, first_lame, shear_modulus, connectivity, owner_list):
    rows, across = lax.axis_size("dom"), lax.axis_size("lvl")
    block, index = pl.pallas_call(
        pack_kernel,
        out_shape=(
            jax.ShapeDtypeStruct((ROWS, LANE), F32),
            jax.ShapeDtypeStruct((32, LANE), jnp.int32),
        ),
        in_specs=[VMEM] * 8,
        out_specs=(VMEM, VMEM),
        scratch_shapes=[pltpu.VMEM((64, 64), jnp.int32)],
        name="pack",
    )(
        displacement,
        velocity,
        inverse_mass.reshape(32, LANE),
        levels.reshape(1, 64),
        first_lame.reshape(1, 64),
        shear_modulus.reshape(1, 64),
        connectivity,
        owner_list.reshape(4, LANE),
    )

    def swap_rows(x, shift):
        pairs = []
        for r in range(rows):
            partner = (r ^ 1) if shift == 0 else (((r - 1) ^ 1) + 1) % rows
            pairs += [(r * across + i, partner * across + i) for i in range(across)]
        return lax.ppermute(x, AXES, pairs)

    def swap_near(x, other):
        pairs = [(r * across + i, r * across + (i ^ other)) for r in range(rows) for i in range(across)]
        return lax.ppermute(x, AXES, pairs)

    even = swap_rows(block, 0)
    odd = swap_rows(block, 1)
    near = [swap_near(block, other) for other in (1, 2, 3)]
    place = pl.pallas_call(
        place_kernel,
        out_shape=jax.ShapeDtypeStruct((64, LANE), jnp.int32),
        in_specs=[VMEM],
        out_specs=VMEM,
        name="place",
        cost_estimate=pl.CostEstimate(flops=67_000_000, bytes_accessed=50_000, transcendentals=0),
    )(index)
    parity = lax.axis_index("dom") % 2
    me = lax.axis_index("lvl")
    give_prev_1 = me % 2 == 1
    give_prev_2 = me >= 2
    prev_is_even = parity == 1
    send_1 = jnp.where(give_prev_1 == prev_is_even, even, odd)
    send_2 = jnp.where(give_prev_2 == prev_is_even, even, odd)
    cross = [swap_near(send_1, 1), swap_near(send_2, 2), swap_near(send_2, 3)]
    flags = jnp.stack([parity, me]).astype(jnp.int32)
    return pl.pallas_call(
        main_kernel,
        out_shape=(
            jax.ShapeDtypeStruct((3, 4096), F32),
            jax.ShapeDtypeStruct((3, 4096), F32),
        ),
        in_specs=[SMEM] + [VMEM] * 10,
        out_specs=(VMEM, VMEM),
        scratch_shapes=[
            pltpu.VMEM((STAGE * SUB, LANE), F32),
            pltpu.VMEM((375 * SUB, LANE), F32),
            pltpu.VMEM((375 * SUB, LANE), F32),
            pltpu.VMEM((375 * SUB, LANE), F32),
            pltpu.VMEM((375 * SUB, LANE), F32),
            pltpu.VMEM((50 * SUB, LANE), F32),
            pltpu.VMEM((6 * 32, LANE), F32),
        ],
        compiler_params=pltpu.CompilerParams(vmem_limit_bytes=40 * 1024 * 1024),
        name="substeps",
    )(flags, block, even, odd, *near, *cross, place)


def solution(mesh):
    both = P(None, AXES)
    flat = P(AXES)
    in_specs = (both, both, flat, flat, flat, flat, both, flat)
    return jax.shard_map(
        per_device, mesh=mesh, in_specs=in_specs, out_specs=(both, both), check_vma=False
    )
```

```python
import jax
import jax.numpy as jnp
import ml_dtypes
import numpy as np
from jax import lax
from jax.experimental import pallas as pl
from jax.experimental.pallas import tpu as pltpu
from jax.sharding import PartitionSpec as P

substep_length = 0.01
AXES = ("dom", "lvl")
SUB, LANE = 8, 128
VALUES = 7
ROWS = VALUES * 32 + 16
COMP = 128
FULL = 3 * COMP
TILES = 5
F32, BF16 = jnp.float32, jnp.bfloat16
WINDOW = ((0, 5, False), (0, 4, True), (0, 4, False), (0, 4, False), (1, 4, False), (1, 3, True), (1, 3, False), (1, 3, False))


def lobatto():
    points = np.array([-1.0, -np.sqrt(3.0 / 7.0), 0.0, np.sqrt(3.0 / 7.0), 1.0])
    weights = np.array([0.1, 49.0 / 90.0, 32.0 / 45.0, 49.0 / 90.0, 0.1])
    factor = np.array(
        [np.prod([points[i] - points[k] for k in range(5) if k != i]) for i in range(5)]
    )
    matrix = np.zeros((5, 5))
    for i in range(5):
        for j in range(5):
            if i == j:
                matrix[i, j] = sum((1.0 / (points[i] - points[k]) for k in range(5) if k != i))
            else:
                matrix[i, j] = factor[i] / (factor[j] * (points[i] - points[j]))
    return matrix, weights


def point_row(a, b, k):
    if a < 4 and b < 4:
        return (k * 16 if k < 4 else 64) + b * 4 + a
    if a < 4:
        return (80 + k * 4 if k < 4 else 120) + a
    if b < 4:
        return 96 + k * 4 + b if k < 4 else 112 + b
    return 116 + k if k < 4 else 124


def element_matrices():
    matrix, weights = lobatto()
    eye = np.eye(5)
    grads = [
        np.einsum("ai,bj,ck->abcijk", *[matrix if x == y else eye for y in range(3)]).reshape(125, 125)
        for x in range(3)
    ]
    cube = np.einsum("a,b,c->abc", weights, weights, weights).reshape(125)
    order = np.array([point_row(a, b, k) for a in range(5) for b in range(5) for k in range(5)])
    both = np.zeros((FULL, 2 * FULL))
    for c in range(3):
        for d in range(3):
            first = grads[c].T @ (cube[:, None] * grads[d])
            shear = grads[d].T @ (cube[:, None] * grads[c])
            if c == d:
                shear = shear + sum(g.T @ (cube[:, None] * g) for g in grads)
            both[np.ix_(c * COMP + order, d * COMP + order)] = first
            both[np.ix_(c * COMP + order, FULL + d * COMP + order)] = shear
    high = both.astype(np.float32).astype(ml_dtypes.bfloat16)
    low = (both - high.astype(np.float64)).astype(np.float32).astype(ml_dtypes.bfloat16)
    return np.concatenate([high, low], axis=0)


def lanes(x, index):
    return jnp.take_along_axis(x, index, axis=1, mode="promise_in_bounds")


def wide(row):
    return jnp.broadcast_to(row, (SUB, LANE))


def as_column(row):
    n = row.shape[1]
    diag = lax.broadcasted_iota(jnp.int32, (n, n), 0) == lax.broadcasted_iota(jnp.int32, (n, n), 1)
    return jnp.sum(jnp.where(diag, jnp.broadcast_to(row, (n, n)), 0.0), axis=1, keepdims=True)


def pack_kernel(u, v, m, lev, lam, mu, conn, own, out, index, stage, aux):
    n = 64
    for i in range(16):
        k, b = i // 4, i % 4
        stage[4 * i : 4 * i + 4, 0:64] = conn[pl.ds(5 * b + k, 4, stride=25), :]
    level = lev[...]
    period = jnp.where(level == 0, 8, jnp.where(level == 1, 4, jnp.where(level == 2, 2, 1)))
    last_corner = conn[100:101, :].astype(F32)
    for i, row in enumerate(
        (conn[0:1, :].astype(F32), conn[4:5, :].astype(F32), conn[20:21, :].astype(F32), last_corner,
         lam[...], mu[...], period.astype(F32))
    ):
        aux[i : i + 1, 0:64] = row
    layer = jnp.where(last_corner >= 4096.0, 1.0, 0.0)
    down = lax.broadcasted_iota(jnp.int32, (n, n), 0)
    across = lax.broadcasted_iota(jnp.int32, (n, n), 1)
    number = down.astype(F32)
    same = (as_column(layer) == layer) & (down < across)
    rank = jnp.sum(jnp.where(same, 1.0, 0.0), axis=0, keepdims=True) + 32.0 * layer
    order = jnp.sum(jnp.where(as_column(rank) == across.astype(F32), number, 0.0), axis=0, keepdims=True)
    order = wide(jnp.concatenate([order, order], axis=1).astype(jnp.int32))
    left = lax.broadcasted_iota(jnp.int32, (SUB, LANE), 1) < 64
    for t in range(4):
        upper = lanes(stage[8 * t : 8 * t + 8, :], order)
        lower = lanes(stage[32 + 8 * t : 40 + 8 * t, :], order)
        index[8 * t : 8 * t + 8, :] = jnp.where(left, upper, lower)
    for t in range(4):
        part = index[8 * t : 8 * t + 8, :]
        high, low = part >> 7, part & 127
        acc = [jnp.zeros((SUB, LANE), F32) for _ in range(VALUES)]
        for r in range(32):
            here = high == r
            for k in range(VALUES):
                if k < 3:
                    row = u[k : k + 1, r * LANE : (r + 1) * LANE]
                elif k < 6:
                    row = v[k - 3 : k - 2, r * LANE : (r + 1) * LANE]
                else:
                    row = m[r : r + 1, :]
                acc[k] = jnp.where(here, lanes(wide(row), low), acc[k])
        for k in range(VALUES):
            out[k * 32 + 8 * t : k * 32 + 8 * t + 8, :] = acc[k]
    out[VALUES * 32 : ROWS, :] = jnp.zeros((16, LANE), F32)
    sorted_aux = lanes(aux[...], order)[:, 0:64]
    corner = {name: sorted_aux[i : i + 1, :] for i, name in enumerate("ozyx")}
    column = {name: as_column(c) for name, c in corner.items()}

    def match(col, row):
        hit = column[col] == corner[row]
        return jnp.sum(jnp.where(hit, number, 0.0), axis=0, keepdims=True)

    slot = jnp.zeros((n, 1), F32)
    for j in range(4):
        count = (lax.broadcasted_iota(jnp.int32, (n, LANE), 1) + (j * LANE + 1)).astype(F32)
        hit = column["o"] == own[j : j + 1, :].astype(F32)
        slot = slot + jnp.sum(jnp.where(hit, count, 0.0), axis=1, keepdims=True)
    slot_row = jnp.sum(jnp.where(down == across, slot, 0.0), axis=0, keepdims=True)
    rows = [
        sorted_aux[4:5, :],
        sorted_aux[5:6, :],
        sorted_aux[6:7, :],
        match("o", "z"),
        match("z", "o"),
        match("o", "y"),
        match("y", "o"),
        match("o", "x"),
        match("x", "o"),
        jnp.where(corner["x"] >= 4096.0, corner["x"] - 4096.0, -1.0),
        jnp.where(slot_row > 0.5, slot_row - 1.0, -2.0),
    ]
    for i, row in enumerate(rows):
        out[VALUES * 32 + i : VALUES * 32 + i + 1, 0:64] = row


def place_kernel(index, place):
    acc = jnp.zeros((64, LANE), F32)
    lane = lax.broadcasted_iota(jnp.int32, (32, LANE), 1).astype(F32)
    sub = lax.broadcasted_iota(jnp.int32, (32, LANE), 0)
    broad = lax.broadcasted_iota(jnp.int32, (LANE, LANE), 0)
    for r in range(32):
        row = index[r : r + 1, :]
        here = sub == (row >> 7)
        left = jnp.concatenate(
            [jnp.where(here, float(r), 0.0), jnp.where(here, lane, 0.0)], axis=0
        ).astype(jnp.bfloat16)
        right = jnp.where(broad == (row & 127), 1.0, 0.0).astype(jnp.bfloat16)
        acc = acc + lax.dot_general(
            left, right, (((1,), (1,)), ((), ())), preferred_element_type=F32
        )
    place[...] = acc.astype(jnp.int32)


def main_kernel(
    flags, own, even, odd, r1, r2, r3, s1, s2, s3, place, matrix, new_u, new_v,
    held, disp, vel, mass, force, high, low, maps, table,
):
    parity, me = flags[0], flags[1]
    lane = lax.broadcasted_iota(jnp.int32, (SUB, LANE), 1)
    sub = lax.broadcasted_iota(jnp.int32, (SUB, LANE), 0)
    left, upper = lane < 64, sub < 4
    is_odd = jnp.full((SUB, LANE), parity, jnp.int32) == 1

    def keep(get, position):
        for r in range(0, ROWS, SUB):
            start = position * ROWS + r
            if not isinstance(start, int):
                start = pl.multiple_of(start, SUB)
            held[pl.ds(start, SUB), :] = get(r)

    keep(lambda r: own[r : r + SUB, :], 4)
    keep(lambda r: jnp.where(is_odd, even[r : r + SUB, :], odd[r : r + SUB, :]), 0)
    keep(lambda r: jnp.where(is_odd, odd[r : r + SUB, :], even[r : r + SUB, :]), 8)
    keep(lambda r: jnp.zeros((SUB, LANE), F32), 9)
    for other, near, cross in ((1, r1, s1), (2, r2, s2), (3, r3, s3)):
        partner = lax.bitwise_xor(me, other)
        away = partner - me
        keep(lambda r, near=near: near[r : r + SUB, :], 4 + away)
        keep(lambda r, cross=cross: cross[r : r + SUB, :], jnp.where(away > 0, away, away + 8))

    step = jnp.float32(substep_length)
    for t in range(TILES):
        for r in range(0, VALUES * 32, SUB):
            x = held[2 * t * ROWS + r : 2 * t * ROWS + r + SUB, :]
            y = held[(2 * t + 1) * ROWS + r : (2 * t + 1) * ROWS + r + SUB, :]
            near = jnp.where(left, x, pltpu.roll(y, 64, 1))
            far = jnp.where(left, pltpu.roll(x, 64, 1), y)
            k, q = r // 32, r % 32
            for p, value in ((q, near), (q + 32, far)):
                if k < 3:
                    row = t * FULL + k * COMP + p
                    disp[row : row + SUB, :] = value
                elif k < 6:
                    row = (t * 3 + k - 3) * 64 + p
                    vel[row : row + SUB, :] = value
                else:
                    row = t * 64 + p
                    mass[row : row + SUB, :] = step * value
        for c in range(3):
            row = t * FULL + c * COMP + 120
            disp[row : row + SUB, :] = jnp.zeros((SUB, LANE), F32)

    def elem(j, i):
        row = j * ROWS + VALUES * 32 + i
        return held[row : row + 1, :]

    ghost = jnp.concatenate([elem(j, 9) for j in range(8)], axis=0)
    corner = jnp.concatenate([elem(j + 1, 10) for j in range(8)], axis=0)
    ghost_t, corner_t = ghost.T, corner.T
    count = lax.broadcasted_iota(jnp.int32, (32, LANE), 0).astype(F32)
    to_next, to_prev = [], []
    for j in range(8):
        hit = corner_t[0:32, j : j + 1] == ghost[j : j + 1, :]
        to_next.append(jnp.sum(jnp.where(hit, count, 0.0), axis=0, keepdims=True))
        hit = ghost_t[32:64, j : j + 1] == corner[j : j + 1, :]
        to_prev.append(jnp.sum(jnp.where(hit, count + 32.0, 0.0), axis=0, keepdims=True))
    none = jnp.zeros((1, LANE), F32)
    to_next += [none, none]
    to_prev = [none] + to_prev + [none]
    half = jnp.where(lane[0:1, :] < 64, 0.0, 64.0)
    first_half = lane[0:1, :] < 64
    layer = (lane[0:1, :] & 63) >= 32

    def join(x, y):
        return jnp.where(first_half, x, pltpu.roll(wide(y), 64, 1)[0:1, :])

    def map_at(t, kind):
        row = (t * 6 + kind) * SUB
        return maps[row : row + SUB, :]

    lame, shear, period = [], [], []
    for t in range(TILES):
        x, y = 2 * t, 2 * t + 1
        lame.append(join(elem(x, 0), elem(y, 0)))
        shear.append(join(elem(x, 1), elem(y, 1)))
        period.append(join(elem(x, 2), elem(y, 2)).astype(jnp.int32))
        rows = [join(elem(x, i), elem(y, i)) + half for i in (3, 4, 5, 6)]
        inside = join(elem(x, 7), elem(y, 7)) + half
        outside = join(to_next[x] + 64.0, to_next[y])
        rows.append(jnp.where(layer, outside, inside))
        inside = join(elem(x, 8), elem(y, 8)) + half
        outside = join(to_prev[x] + 64.0, to_prev[y])
        rows.append(jnp.where(layer, inside, outside))
        for kind, row in enumerate(rows):
            maps[(t * 6 + kind) * SUB : (t * 6 + kind + 1) * SUB, :] = wide(row.astype(jnp.int32))

    def faces(t):
        for c in range(3):
            o = t * FULL + c * COMP
            for r in (0, 8):
                disp[o + 64 + r : o + 72 + r, :] = lanes(disp[o + r : o + r + 8, :], map_at(t, 0))
        for c in range(3):
            o = t * FULL + c * COMP
            for r in (0, 32):
                x = jnp.where(upper, disp[o + r : o + r + 8, :], disp[o + r + 12 : o + r + 20, :])
                to = o + 80 + r // 4
                disp[to : to + 8, :] = lanes(x, map_at(t, 2))
        o = t * FULL
        x = jnp.where(upper, disp[o + 64 : o + 72, :], disp[o + COMP + 60 : o + COMP + 68, :])
        x = lanes(x, map_at(t, 2))
        disp[o + 120 : o + 124, :] = x[0:4, :]
        disp[o + COMP + 120 : o + COMP + 124, :] = x[4:8, :]
        o = o + 2 * COMP
        disp[o + 120 : o + 124, :] = lanes(disp[o + 64 : o + 72, :], map_at(t, 2))[0:4, :]

    def corners(ref, t, row):
        o = t * FULL + row
        x = jnp.where(sub == 1, ref[o + COMP - 1 : o + COMP + 7, :], ref[o + 2 * COMP - 2 : o + 2 * COMP + 6, :])
        return jnp.where(sub == 0, ref[o : o + 8, :], x)

    def ahead(t, following):
        def pick(x, y):
            return lanes(jnp.where(lane < 32, y, x), map_at(t, 4))

        for c in range(3):
            for i in range(3):
                x = disp[pl.ds(t * FULL + c * COMP + 32 * i, SUB, stride=4), :]
                y = disp[pl.ds(following * FULL + c * COMP + 32 * i, SUB, stride=4), :]
                to = t * FULL + c * COMP + 96 + 8 * i
                disp[to : to + 8, :] = pick(x, y)
        x = pick(corners(disp, t, 120), corners(disp, following, 120))
        for c in range(3):
            row = t * FULL + c * COMP + 124
            disp[row : row + 1, :] = x[c : c + 1, :]

    def collect(t, before):
        def pick(x, y):
            return lanes(jnp.where(lane >= 96, y, x), map_at(t, 5))

        for c in range(3):
            for i in range(3):
                row = t * FULL + c * COMP + 96 + 8 * i
                other = before * FULL + c * COMP + 96 + 8 * i
                x = pick(force[row : row + 8, :], force[other : other + 8, :])
                where = pl.ds(t * FULL + c * COMP + 32 * i, SUB, stride=4)
                force[where, :] = force[where, :] + x
        o, w = t * FULL + 120, before * FULL + 120
        mine = jnp.concatenate([force[o + c * COMP + 4 : o + c * COMP + 5, :] for c in range(3)] + [wide(none)[0:5, :]], axis=0)
        theirs = jnp.concatenate([force[w + c * COMP + 4 : w + c * COMP + 5, :] for c in range(3)] + [wide(none)[0:5, :]], axis=0)
        x = pick(mine, theirs)
        for c in range(3):
            row = o + c * COMP
            force[row : row + 1, :] = force[row : row + 1, :] + x[c : c + 1, :]
        for c in range(3):
            o = t * FULL + c * COMP
            for r in (0, 32):
                row = o + 80 + r // 4
                x = lanes(force[row : row + 8, :], map_at(t, 3))
                force[o + r : o + r + 4, :] = force[o + r : o + r + 4, :] + x[0:4, :]
                force[o + r + 16 : o + r + 20, :] = force[o + r + 16 : o + r + 20, :] + x[4:8, :]
            x = lanes(force[o + 120 : o + 128, :], map_at(t, 3))
            force[o + 64 : o + 68, :] = force[o + 64 : o + 68, :] + x[0:4, :]
        for c in range(3):
            o = t * FULL + c * COMP
            for r in range(0, 64, SUB):
                f = force[o + r : o + r + 8, :]
                if r < 16:
                    f = f + lanes(force[o + 64 + r : o + 72 + r, :], map_at(t, 1))
                row = (t * 3 + c) * 64 + r
                speed = vel[row : row + 8, :] - mass[t * 64 + r : t * 64 + r + 8, :] * f
                vel[row : row + 8, :] = speed
                disp[o + r : o + r + 8, :] = disp[o + r : o + r + 8, :] + step * speed

    for s, (begin, end, extra) in enumerate(WINDOW):
        for t in range(begin, end + (1 if extra else 0)):
            faces(t)
        for t in range(begin, end):
            ahead(t, t + 1 if t + 1 < end or extra else t)
            weight = jnp.where((s & (period[t] - 1)) == 0, period[t], 0).astype(F32)
            u = disp[t * FULL : (t + 1) * FULL, :]
            for i, factor in enumerate((lame[t] * weight, shear[t] * weight)):
                x = u * factor
                head = x.astype(BF16)
                high[i * FULL : (i + 1) * FULL, t * LANE : (t + 1) * LANE] = head
                low[i * FULL : (i + 1) * FULL, t * LANE : (t + 1) * LANE] = (x - head.astype(F32)).astype(BF16)
        span = slice(begin * LANE, end * LANE)
        head = high[:, span]
        both = jnp.dot(matrix[...], head, preferred_element_type=F32)
        total = both[0:FULL] + both[FULL:] + jnp.dot(matrix[0:FULL, :], low[:, span], preferred_element_type=F32)
        for t in range(begin, end):
            force[t * FULL : (t + 1) * FULL, :] = total[:, (t - begin) * LANE : (t - begin + 1) * LANE]
        for t in range(begin, end):
            collect(t, t - 1 if t > begin else t)

    for c in range(3):
        for q in range(0, 32, SUB):
            row = 2 * FULL + c * COMP + q
            x, y = disp[row : row + 8, :], disp[row + 32 : row + 40, :]
            table[c * 32 + q : c * 32 + q + 8, :] = jnp.where(left, x, pltpu.roll(y, 64, 1))
            row = (6 + c) * 64 + q
            x, y = vel[row : row + 8, :], vel[row + 32 : row + 40, :]
            table[(3 + c) * 32 + q : (3 + c) * 32 + q + 8, :] = jnp.where(left, x, pltpu.roll(y, 64, 1))
    for t in range(4):
        row, column = place[8 * t : 8 * t + 8, :], place[32 + 8 * t : 32 + 8 * t + 8, :]
        acc = [jnp.zeros((SUB, LANE), F32) for _ in range(6)]
        for q in range(32):
            here = row == q
            for k in range(6):
                value = lanes(wide(table[k * 32 + q : k * 32 + q + 1, :]), column)
                acc[k] = jnp.where(here, value, acc[k])
        for k in range(6):
            for j in range(SUB):
                n = (8 * t + j) * LANE
                ref = new_u if k < 3 else new_v
                ref[k % 3 : k % 3 + 1, n : n + LANE] = acc[k][j : j + 1, :]


VMEM = pl.BlockSpec(memory_space=pltpu.VMEM)
SMEM = pl.BlockSpec(memory_space=pltpu.SMEM)


def main_call():
    return pl.pallas_call(
        main_kernel,
        out_shape=(
            jax.ShapeDtypeStruct((3, 4096), F32),
            jax.ShapeDtypeStruct((3, 4096), F32),
        ),
        in_specs=[SMEM] + [VMEM] * 11,
        out_specs=(VMEM, VMEM),
        scratch_shapes=[
            pltpu.VMEM((10 * ROWS, LANE), F32),
            pltpu.VMEM((TILES * FULL, LANE), F32),
            pltpu.VMEM((TILES * 3 * 64, LANE), F32),
            pltpu.VMEM((TILES * 64, LANE), F32),
            pltpu.VMEM((TILES * FULL, LANE), F32),
            pltpu.VMEM((2 * FULL, TILES * LANE), BF16),
            pltpu.VMEM((2 * FULL, TILES * LANE), BF16),
            pltpu.VMEM((TILES * 6 * SUB, LANE), jnp.int32),
            pltpu.VMEM((6 * 32, LANE), F32),
        ],
        compiler_params=pltpu.CompilerParams(vmem_limit_bytes=40 * 1024 * 1024),
        name="substeps",
    )


def per_device(displacement, velocity, inverse_mass, levels, first_lame, shear_modulus, connectivity, owner_list):
    rows, across = lax.axis_size("dom"), lax.axis_size("lvl")
    block, index = pl.pallas_call(
        pack_kernel,
        out_shape=(
            jax.ShapeDtypeStruct((ROWS, LANE), F32),
            jax.ShapeDtypeStruct((32, LANE), jnp.int32),
        ),
        in_specs=[VMEM] * 8,
        out_specs=(VMEM, VMEM),
        scratch_shapes=[pltpu.VMEM((64, LANE), jnp.int32), pltpu.VMEM((SUB, LANE), F32)],
        name="pack",
    )(
        displacement,
        velocity,
        inverse_mass.reshape(32, LANE),
        levels.reshape(1, 64),
        first_lame.reshape(1, 64),
        shear_modulus.reshape(1, 64),
        connectivity,
        owner_list.reshape(4, LANE),
    )

    def swap_rows(x, shift):
        pairs = []
        for r in range(rows):
            partner = (r ^ 1) if shift == 0 else (((r - 1) ^ 1) + 1) % rows
            pairs += [(r * across + i, partner * across + i) for i in range(across)]
        return lax.ppermute(x, AXES, pairs)

    def swap_near(x, other):
        pairs = [(r * across + i, r * across + (i ^ other)) for r in range(rows) for i in range(across)]
        return lax.ppermute(x, AXES, pairs)

    even = swap_rows(block, 0)
    odd = swap_rows(block, 1)
    near = [swap_near(block, other) for other in (1, 2, 3)]
    place = pl.pallas_call(
        place_kernel,
        out_shape=jax.ShapeDtypeStruct((64, LANE), jnp.int32),
        in_specs=[VMEM],
        out_specs=VMEM,
        name="place",
        cost_estimate=pl.CostEstimate(flops=67_000_000, bytes_accessed=50_000, transcendentals=0),
    )(index)
    parity = lax.axis_index("dom") % 2
    me = lax.axis_index("lvl")
    give_prev_1 = me % 2 == 1
    give_prev_2 = me >= 2
    prev_is_even = parity == 1
    send_1 = jnp.where(give_prev_1 == prev_is_even, even, odd)
    send_2 = jnp.where(give_prev_2 == prev_is_even, even, odd)
    cross = [swap_near(send_1, 1), swap_near(send_2, 2), swap_near(send_2, 3)]
    flags = jnp.stack([parity, me]).astype(jnp.int32)
    return main_call()(flags, block, even, odd, *near, *cross, place, jnp.asarray(element_matrices()))


def solution(mesh):
    both = P(None, AXES)
    flat = P(AXES)
    in_specs = (both, both, flat, flat, flat, flat, both, flat)
    return jax.shard_map(
        per_device, mesh=mesh, in_specs=in_specs, out_specs=(both, both), check_vma=False
    )
```

```python
import jax
import jax.numpy as jnp
import ml_dtypes
import numpy as np
from jax import lax
from jax.experimental import pallas as pl
from jax.experimental.pallas import tpu as pltpu
from jax.sharding import PartitionSpec as P

substep_length = 0.01
AXES = ("dom", "lvl")
SUB, LANE = 8, 128
VALUES = 7
ROWS = VALUES * 32 + 16
COMP = 128
FULL = 3 * COMP
TILES = 5
F32, BF16 = jnp.float32, jnp.bfloat16
WINDOW = ((0, 5, False), (0, 4, True), (0, 4, False), (0, 4, False), (1, 4, False), (1, 3, True), (1, 3, False), (1, 3, False))


def lobatto():
    points = np.array([-1.0, -np.sqrt(3.0 / 7.0), 0.0, np.sqrt(3.0 / 7.0), 1.0])
    weights = np.array([0.1, 49.0 / 90.0, 32.0 / 45.0, 49.0 / 90.0, 0.1])
    factor = np.array(
        [np.prod([points[i] - points[k] for k in range(5) if k != i]) for i in range(5)]
    )
    matrix = np.zeros((5, 5))
    for i in range(5):
        for j in range(5):
            if i == j:
                matrix[i, j] = sum((1.0 / (points[i] - points[k]) for k in range(5) if k != i))
            else:
                matrix[i, j] = factor[i] / (factor[j] * (points[i] - points[j]))
    return matrix, weights


def point_row(a, b, k):
    if a < 4 and b < 4:
        return (k * 16 if k < 4 else 64) + b * 4 + a
    if a < 4:
        return (80 + k * 4 if k < 4 else 120) + a
    if b < 4:
        return 96 + k * 4 + b if k < 4 else 112 + b
    return 116 + k if k < 4 else 124


def element_matrices():
    matrix, weights = lobatto()
    eye = np.eye(5)
    grads = [
        np.einsum("ai,bj,ck->abcijk", *[matrix if x == y else eye for y in range(3)]).reshape(125, 125)
        for x in range(3)
    ]
    cube = np.einsum("a,b,c->abc", weights, weights, weights).reshape(125)
    order = np.array([point_row(a, b, k) for a in range(5) for b in range(5) for k in range(5)])
    both = np.zeros((FULL, 2 * FULL))
    for c in range(3):
        for d in range(3):
            first = grads[c].T @ (cube[:, None] * grads[d])
            shear = grads[d].T @ (cube[:, None] * grads[c])
            if c == d:
                shear = shear + sum(g.T @ (cube[:, None] * g) for g in grads)
            both[np.ix_(c * COMP + order, d * COMP + order)] = first
            both[np.ix_(c * COMP + order, FULL + d * COMP + order)] = shear
    high = both.astype(np.float32).astype(ml_dtypes.bfloat16)
    low = (both - high.astype(np.float64)).astype(np.float32).astype(ml_dtypes.bfloat16)
    return np.concatenate([high, low], axis=0)


def lanes(x, index):
    return jnp.take_along_axis(x, index, axis=1, mode="promise_in_bounds")


def wide(row):
    return jnp.broadcast_to(row, (SUB, LANE))


def as_column(row):
    n = row.shape[1]
    diag = lax.broadcasted_iota(jnp.int32, (n, n), 0) == lax.broadcasted_iota(jnp.int32, (n, n), 1)
    return jnp.sum(jnp.where(diag, jnp.broadcast_to(row, (n, n)), 0.0), axis=1, keepdims=True)


def pack_kernel(u, v, m, lev, lam, mu, stored, own, out, index, stage, aux, turned, conn):
    n = 64
    turned[:, 0:125] = stored[...].astype(F32)
    conn[...] = turned[...].T.astype(jnp.int32)
    for i in range(16):
        k, b = i // 4, i % 4
        stage[4 * i : 4 * i + 4, 0:64] = conn[pl.ds(5 * b + k, 4, stride=25), :]
    level = lev[...]
    period = jnp.where(level == 0, 8, jnp.where(level == 1, 4, jnp.where(level == 2, 2, 1)))
    last_corner = conn[100:101, :].astype(F32)
    for i, row in enumerate(
        (conn[0:1, :].astype(F32), conn[4:5, :].astype(F32), conn[20:21, :].astype(F32), last_corner,
         lam[...], mu[...], period.astype(F32))
    ):
        aux[i : i + 1, 0:64] = row
    layer = jnp.where(last_corner >= 4096.0, 1.0, 0.0)
    down = lax.broadcasted_iota(jnp.int32, (n, n), 0)
    across = lax.broadcasted_iota(jnp.int32, (n, n), 1)
    number = down.astype(F32)
    same = (as_column(layer) == layer) & (down < across)
    rank = jnp.sum(jnp.where(same, 1.0, 0.0), axis=0, keepdims=True) + 32.0 * layer
    order = jnp.sum(jnp.where(as_column(rank) == across.astype(F32), number, 0.0), axis=0, keepdims=True)
    order = wide(jnp.concatenate([order, order], axis=1).astype(jnp.int32))
    left = lax.broadcasted_iota(jnp.int32, (SUB, LANE), 1) < 64
    for t in range(4):
        upper = lanes(stage[8 * t : 8 * t + 8, :], order)
        lower = lanes(stage[32 + 8 * t : 40 + 8 * t, :], order)
        index[8 * t : 8 * t + 8, :] = jnp.where(left, upper, lower)
    for t in range(4):
        part = index[8 * t : 8 * t + 8, :]
        high, low = part >> 7, part & 127
        acc = [jnp.zeros((SUB, LANE), F32) for _ in range(VALUES)]
        for r in range(32):
            here = high == r
            for k in range(VALUES):
                if k < 3:
                    row = u[k : k + 1, r * LANE : (r + 1) * LANE]
                elif k < 6:
                    row = v[k - 3 : k - 2, r * LANE : (r + 1) * LANE]
                else:
                    row = m[r : r + 1, :]
                acc[k] = jnp.where(here, lanes(wide(row), low), acc[k])
        for k in range(VALUES):
            out[k * 32 + 8 * t : k * 32 + 8 * t + 8, :] = acc[k]
    out[VALUES * 32 : ROWS, :] = jnp.zeros((16, LANE), F32)
    sorted_aux = lanes(aux[...], order)[:, 0:64]
    corner = {name: sorted_aux[i : i + 1, :] for i, name in enumerate("ozyx")}
    column = {name: as_column(c) for name, c in corner.items()}

    def match(col, row):
        hit = column[col] == corner[row]
        return jnp.sum(jnp.where(hit, number, 0.0), axis=0, keepdims=True)

    slot = jnp.zeros((n, 1), F32)
    for j in range(4):
        count = (lax.broadcasted_iota(jnp.int32, (n, LANE), 1) + (j * LANE + 1)).astype(F32)
        hit = column["o"] == own[j : j + 1, :].astype(F32)
        slot = slot + jnp.sum(jnp.where(hit, count, 0.0), axis=1, keepdims=True)
    slot_row = jnp.sum(jnp.where(down == across, slot, 0.0), axis=0, keepdims=True)
    rows = [
        sorted_aux[4:5, :],
        sorted_aux[5:6, :],
        sorted_aux[6:7, :],
        match("o", "z"),
        match("z", "o"),
        match("o", "y"),
        match("y", "o"),
        match("o", "x"),
        match("x", "o"),
        jnp.where(corner["x"] >= 4096.0, corner["x"] - 4096.0, -1.0),
        jnp.where(slot_row > 0.5, slot_row - 1.0, -2.0),
    ]
    for i, row in enumerate(rows):
        out[VALUES * 32 + i : VALUES * 32 + i + 1, 0:64] = row


def place_kernel(index, place):
    acc = jnp.zeros((64, LANE), F32)
    lane = lax.broadcasted_iota(jnp.int32, (32, LANE), 1).astype(F32)
    sub = lax.broadcasted_iota(jnp.int32, (32, LANE), 0)
    broad = lax.broadcasted_iota(jnp.int32, (LANE, LANE), 0)
    for r in range(32):
        row = index[r : r + 1, :]
        here = sub == (row >> 7)
        left = jnp.concatenate(
            [jnp.where(here, float(r), 0.0), jnp.where(here, lane, 0.0)], axis=0
        ).astype(jnp.bfloat16)
        right = jnp.where(broad == (row & 127), 1.0, 0.0).astype(jnp.bfloat16)
        acc = acc + lax.dot_general(
            left, right, (((1,), (1,)), ((), ())), preferred_element_type=F32
        )
    place[...] = acc.astype(jnp.int32)


def main_kernel(
    flags, own_far, even, odd, r1, r2, r3, s1, s2, s3, place_far, matrix_far, new_u, new_v,
    held, disp, vel, mass, force, high, low, maps, table, own, place, matrix, sems,
):
    parity, me = flags[0], flags[1]
    lane = lax.broadcasted_iota(jnp.int32, (SUB, LANE), 1)
    sub = lax.broadcasted_iota(jnp.int32, (SUB, LANE), 0)
    left, upper = lane < 64, sub < 4
    is_odd = jnp.full((SUB, LANE), parity, jnp.int32) == 1

    def keep(get, position):
        for r in range(0, ROWS, SUB):
            start = position * ROWS + r
            if not isinstance(start, int):
                start = pl.multiple_of(start, SUB)
            held[pl.ds(start, SUB), :] = get(r)

    copies = [
        pltpu.make_async_copy(far, near, sems.at[i])
        for i, (far, near) in enumerate(((own_far, own), (matrix_far, matrix), (place_far, place)))
    ]
    for copy in copies:
        copy.start()
    keep(lambda r: jnp.where(is_odd, even[r : r + SUB, :], odd[r : r + SUB, :]), 0)
    keep(lambda r: jnp.where(is_odd, odd[r : r + SUB, :], even[r : r + SUB, :]), 8)
    keep(lambda r: jnp.zeros((SUB, LANE), F32), 9)
    for other, near, cross in ((1, r1, s1), (2, r2, s2), (3, r3, s3)):
        partner = lax.bitwise_xor(me, other)
        away = partner - me
        keep(lambda r, near=near: near[r : r + SUB, :], 4 + away)
        keep(lambda r, cross=cross: cross[r : r + SUB, :], jnp.where(away > 0, away, away + 8))
    copies[0].wait()
    keep(lambda r: own[r : r + SUB, :], 4)

    step = jnp.float32(substep_length)
    for t in range(TILES):
        for r in range(0, VALUES * 32, SUB):
            x = held[2 * t * ROWS + r : 2 * t * ROWS + r + SUB, :]
            y = held[(2 * t + 1) * ROWS + r : (2 * t + 1) * ROWS + r + SUB, :]
            near = jnp.where(left, x, pltpu.roll(y, 64, 1))
            far = jnp.where(left, pltpu.roll(x, 64, 1), y)
            k, q = r // 32, r % 32
            for p, value in ((q, near), (q + 32, far)):
                if k < 3:
                    row = t * FULL + k * COMP + p
                    disp[row : row + SUB, :] = value
                elif k < 6:
                    row = (t * 3 + k - 3) * 64 + p
                    vel[row : row + SUB, :] = value
                else:
                    row = t * 64 + p
                    mass[row : row + SUB, :] = step * value
        for c in range(3):
            row = t * FULL + c * COMP + 120
            disp[row : row + SUB, :] = jnp.zeros((SUB, LANE), F32)

    def elem(j, i):
        row = j * ROWS + VALUES * 32 + i
        return held[row : row + 1, :]

    ghost = jnp.concatenate([elem(j, 9) for j in range(8)], axis=0)
    corner = jnp.concatenate([elem(j + 1, 10) for j in range(8)], axis=0)
    ghost_t, corner_t = ghost.T, corner.T
    count = lax.broadcasted_iota(jnp.int32, (32, LANE), 0).astype(F32)
    to_next, to_prev = [], []
    for j in range(8):
        hit = corner_t[0:32, j : j + 1] == ghost[j : j + 1, :]
        to_next.append(jnp.sum(jnp.where(hit, count, 0.0), axis=0, keepdims=True))
        hit = ghost_t[32:64, j : j + 1] == corner[j : j + 1, :]
        to_prev.append(jnp.sum(jnp.where(hit, count + 32.0, 0.0), axis=0, keepdims=True))
    none = jnp.zeros((1, LANE), F32)
    to_next += [none, none]
    to_prev = [none] + to_prev + [none]
    half = jnp.where(lane[0:1, :] < 64, 0.0, 64.0)
    first_half = lane[0:1, :] < 64
    layer = (lane[0:1, :] & 63) >= 32

    def join(x, y):
        return jnp.where(first_half, x, pltpu.roll(wide(y), 64, 1)[0:1, :])

    def map_at(t, kind):
        row = (t * 6 + kind) * SUB
        return maps[row : row + SUB, :]

    lame, shear, period = [], [], []
    for t in range(TILES):
        x, y = 2 * t, 2 * t + 1
        lame.append(join(elem(x, 0), elem(y, 0)))
        shear.append(join(elem(x, 1), elem(y, 1)))
        period.append(join(elem(x, 2), elem(y, 2)).astype(jnp.int32))
        rows = [join(elem(x, i), elem(y, i)) + half for i in (3, 4, 5, 6)]
        inside = join(elem(x, 7), elem(y, 7)) + half
        outside = join(to_next[x] + 64.0, to_next[y])
        rows.append(jnp.where(layer, outside, inside))
        inside = join(elem(x, 8), elem(y, 8)) + half
        outside = join(to_prev[x] + 64.0, to_prev[y])
        rows.append(jnp.where(layer, inside, outside))
        for kind, row in enumerate(rows):
            maps[(t * 6 + kind) * SUB : (t * 6 + kind + 1) * SUB, :] = wide(row.astype(jnp.int32))

    def faces(t):
        for c in range(3):
            o = t * FULL + c * COMP
            for r in (0, 8):
                disp[o + 64 + r : o + 72 + r, :] = lanes(disp[o + r : o + r + 8, :], map_at(t, 0))
        for c in range(3):
            o = t * FULL + c * COMP
            for r in (0, 32):
                x = jnp.where(upper, disp[o + r : o + r + 8, :], disp[o + r + 12 : o + r + 20, :])
                to = o + 80 + r // 4
                disp[to : to + 8, :] = lanes(x, map_at(t, 2))
        o = t * FULL
        x = jnp.where(upper, disp[o + 64 : o + 72, :], disp[o + COMP + 60 : o + COMP + 68, :])
        x = lanes(x, map_at(t, 2))
        disp[o + 120 : o + 124, :] = x[0:4, :]
        disp[o + COMP + 120 : o + COMP + 124, :] = x[4:8, :]
        o = o + 2 * COMP
        disp[o + 120 : o + 124, :] = lanes(disp[o + 64 : o + 72, :], map_at(t, 2))[0:4, :]

    def corners(ref, t, row):
        o = t * FULL + row
        x = jnp.where(sub == 1, ref[o + COMP - 1 : o + COMP + 7, :], ref[o + 2 * COMP - 2 : o + 2 * COMP + 6, :])
        return jnp.where(sub == 0, ref[o : o + 8, :], x)

    def ahead(t, following):
        def pick(x, y):
            return lanes(jnp.where(lane < 32, y, x), map_at(t, 4))

        for c in range(3):
            for i in range(3):
                x = disp[pl.ds(t * FULL + c * COMP + 32 * i, SUB, stride=4), :]
                y = disp[pl.ds(following * FULL + c * COMP + 32 * i, SUB, stride=4), :]
                to = t * FULL + c * COMP + 96 + 8 * i
                disp[to : to + 8, :] = pick(x, y)
        x = pick(corners(disp, t, 120), corners(disp, following, 120))
        for c in range(3):
            row = t * FULL + c * COMP + 124
            disp[row : row + 1, :] = x[c : c + 1, :]

    def collect(t, before):
        def pick(x, y):
            return lanes(jnp.where(lane >= 96, y, x), map_at(t, 5))

        for c in range(3):
            for i in range(3):
                row = t * FULL + c * COMP + 96 + 8 * i
                other = before * FULL + c * COMP + 96 + 8 * i
                x = pick(force[row : row + 8, :], force[other : other + 8, :])
                where = pl.ds(t * FULL + c * COMP + 32 * i, SUB, stride=4)
                force[where, :] = force[where, :] + x
        o, w = t * FULL + 120, before * FULL + 120
        mine = jnp.concatenate([force[o + c * COMP + 4 : o + c * COMP + 5, :] for c in range(3)] + [wide(none)[0:5, :]], axis=0)
        theirs = jnp.concatenate([force[w + c * COMP + 4 : w + c * COMP + 5, :] for c in range(3)] + [wide(none)[0:5, :]], axis=0)
        x = pick(mine, theirs)
        for c in range(3):
            row = o + c * COMP
            force[row : row + 1, :] = force[row : row + 1, :] + x[c : c + 1, :]
        for c in range(3):
            o = t * FULL + c * COMP
            for r in (0, 32):
                row = o + 80 + r // 4
                x = lanes(force[row : row + 8, :], map_at(t, 3))
                force[o + r : o + r + 4, :] = force[o + r : o + r + 4, :] + x[0:4, :]
                force[o + r + 16 : o + r + 20, :] = force[o + r + 16 : o + r + 20, :] + x[4:8, :]
            x = lanes(force[o + 120 : o + 128, :], map_at(t, 3))
            force[o + 64 : o + 68, :] = force[o + 64 : o + 68, :] + x[0:4, :]
        for c in range(3):
            o = t * FULL + c * COMP
            for r in range(0, 64, SUB):
                f = force[o + r : o + r + 8, :]
                if r < 16:
                    f = f + lanes(force[o + 64 + r : o + 72 + r, :], map_at(t, 1))
                row = (t * 3 + c) * 64 + r
                speed = vel[row : row + 8, :] - mass[t * 64 + r : t * 64 + r + 8, :] * f
                vel[row : row + 8, :] = speed
                disp[o + r : o + r + 8, :] = disp[o + r : o + r + 8, :] + step * speed

    copies[1].wait()
    for s, (begin, end, extra) in enumerate(WINDOW):
        for t in range(begin, end + (1 if extra else 0)):
            faces(t)
        groups = [(g, min(g + 2, end)) for g in range(begin, end, 2)]
        for first, last_tile in groups:
            for t in range(first, last_tile):
                ahead(t, t + 1 if t + 1 < end or extra else t)
                weight = jnp.where((s & (period[t] - 1)) == 0, period[t], 0).astype(F32)
                u = disp[t * FULL : (t + 1) * FULL, :]
                for i, factor in enumerate((lame[t] * weight, shear[t] * weight)):
                    x = u * factor
                    head = x.astype(BF16)
                    high[i * FULL : (i + 1) * FULL, t * LANE : (t + 1) * LANE] = head
                    low[i * FULL : (i + 1) * FULL, t * LANE : (t + 1) * LANE] = (x - head.astype(F32)).astype(BF16)
            span = slice(first * LANE, last_tile * LANE)
            both = jnp.dot(matrix[...], high[:, span], preferred_element_type=F32)
            total = both[0:FULL] + both[FULL:] + jnp.dot(matrix[0:FULL, :], low[:, span], preferred_element_type=F32)
            for t in range(first, last_tile):
                force[t * FULL : (t + 1) * FULL, :] = total[:, (t - first) * LANE : (t - first + 1) * LANE]
        for t in range(begin, end):
            collect(t, t - 1 if t > begin else t)

    for c in range(3):
        for q in range(0, 32, SUB):
            row = 2 * FULL + c * COMP + q
            x, y = disp[row : row + 8, :], disp[row + 32 : row + 40, :]
            table[c * 32 + q : c * 32 + q + 8, :] = jnp.where(left, x, pltpu.roll(y, 64, 1))
            row = (6 + c) * 64 + q
            x, y = vel[row : row + 8, :], vel[row + 32 : row + 40, :]
            table[(3 + c) * 32 + q : (3 + c) * 32 + q + 8, :] = jnp.where(left, x, pltpu.roll(y, 64, 1))
    copies[2].wait()
    for t in range(4):
        row, column = place[8 * t : 8 * t + 8, :], place[32 + 8 * t : 32 + 8 * t + 8, :]
        acc = [jnp.zeros((SUB, LANE), F32) for _ in range(6)]
        for q in range(32):
            here = row == q
            for k in range(6):
                value = lanes(wide(table[k * 32 + q : k * 32 + q + 1, :]), column)
                acc[k] = jnp.where(here, value, acc[k])
        for k in range(6):
            for j in range(SUB):
                n = (8 * t + j) * LANE
                ref = new_u if k < 3 else new_v
                ref[k % 3 : k % 3 + 1, n : n + LANE] = acc[k][j : j + 1, :]


VMEM = pl.BlockSpec(memory_space=pltpu.VMEM)
SMEM = pl.BlockSpec(memory_space=pltpu.SMEM)
FAR = pl.BlockSpec(memory_space=pltpu.HBM)


def main_call():
    return pl.pallas_call(
        main_kernel,
        out_shape=(
            jax.ShapeDtypeStruct((3, 4096), F32),
            jax.ShapeDtypeStruct((3, 4096), F32),
        ),
        in_specs=[SMEM, FAR] + [VMEM] * 8 + [FAR, FAR],
        out_specs=(VMEM, VMEM),
        scratch_shapes=[
            pltpu.VMEM((10 * ROWS, LANE), F32),
            pltpu.VMEM((TILES * FULL, LANE), F32),
            pltpu.VMEM((TILES * 3 * 64, LANE), F32),
            pltpu.VMEM((TILES * 64, LANE), F32),
            pltpu.VMEM((TILES * FULL, LANE), F32),
            pltpu.VMEM((2 * FULL, TILES * LANE), BF16),
            pltpu.VMEM((2 * FULL, TILES * LANE), BF16),
            pltpu.VMEM((TILES * 6 * SUB, LANE), jnp.int32),
            pltpu.VMEM((6 * 32, LANE), F32),
            pltpu.VMEM((ROWS, LANE), F32),
            pltpu.VMEM((64, LANE), jnp.int32),
            pltpu.VMEM((2 * FULL, 2 * FULL), BF16),
            pltpu.SemaphoreType.DMA((3,)),
        ],
        compiler_params=pltpu.CompilerParams(vmem_limit_bytes=40 * 1024 * 1024),
        name="substeps",
    )


def per_device(displacement, velocity, inverse_mass, levels, first_lame, shear_modulus, connectivity, owner_list):
    rows, across = lax.axis_size("dom"), lax.axis_size("lvl")
    block, index = pl.pallas_call(
        pack_kernel,
        out_shape=(
            jax.ShapeDtypeStruct((ROWS, LANE), F32),
            jax.ShapeDtypeStruct((32, LANE), jnp.int32),
        ),
        in_specs=[VMEM] * 8,
        out_specs=(VMEM, VMEM),
        scratch_shapes=[pltpu.VMEM((64, LANE), jnp.int32), pltpu.VMEM((SUB, LANE), F32),
            pltpu.VMEM((64, LANE), F32), pltpu.VMEM((LANE, 64), jnp.int32)],
        name="pack",
    )(
        displacement,
        velocity,
        inverse_mass.reshape(32, LANE),
        levels.reshape(1, 64),
        first_lame.reshape(1, 64),
        shear_modulus.reshape(1, 64),
        connectivity.T,
        owner_list.reshape(4, LANE),
    )

    def swap_rows(x, shift):
        pairs = []
        for r in range(rows):
            partner = (r ^ 1) if shift == 0 else (((r - 1) ^ 1) + 1) % rows
            pairs += [(r * across + i, partner * across + i) for i in range(across)]
        return lax.ppermute(x, AXES, pairs)

    def swap_near(x, other):
        pairs = [(r * across + i, r * across + (i ^ other)) for r in range(rows) for i in range(across)]
        return lax.ppermute(x, AXES, pairs)

    near = [swap_near(block, other) for other in (1, 2, 3)]
    even = swap_rows(block, 0)
    odd = swap_rows(block, 1)
    matrix = jnp.asarray(element_matrices())
    odd, even, near, matrix = lax.optimization_barrier((odd, even, near, matrix))
    place = pl.pallas_call(
        place_kernel,
        out_shape=jax.ShapeDtypeStruct((64, LANE), jnp.int32),
        in_specs=[VMEM],
        out_specs=VMEM,
        name="place",
        cost_estimate=pl.CostEstimate(flops=67_000_000, bytes_accessed=50_000, transcendentals=0),
    )(index)
    even, odd, place = lax.optimization_barrier((even, odd, place))
    parity = lax.axis_index("dom") % 2
    me = lax.axis_index("lvl")
    give_prev_1 = me % 2 == 1
    give_prev_2 = me >= 2
    prev_is_even = parity == 1
    send_1 = jnp.where(give_prev_1 == prev_is_even, even, odd)
    send_2 = jnp.where(give_prev_2 == prev_is_even, even, odd)
    cross = [swap_near(send_1, 1), swap_near(send_2, 2), swap_near(send_2, 3)]
    flags = jnp.stack([parity, me]).astype(jnp.int32)
    hold = lambda x: pltpu.with_memory_space_constraint(x, pltpu.HBM)
    return main_call()(flags, hold(block), even, odd, *near, *cross, hold(place), hold(matrix))


def solution(mesh):
    both = P(None, AXES)
    flat = P(AXES)
    in_specs = (both, both, flat, flat, flat, flat, both, flat)
    return jax.shard_map(
        per_device, mesh=mesh, in_specs=in_specs, out_specs=(both, both), check_vma=False
    )
```

```python
import jax
import jax.numpy as jnp
import ml_dtypes
import numpy as np
from jax import lax
from jax.experimental import pallas as pl
from jax.experimental.pallas import tpu as pltpu
from jax.sharding import PartitionSpec as P

substep_length = 0.01
AXES = ("dom", "lvl")
SUB, LANE = 8, 128
VALUES = 7
ROWS = VALUES * 32 + 16
COMP = 128
FULL = 3 * COMP
TILES = 5
F32, BF16 = jnp.float32, jnp.bfloat16
WINDOW = ((0, 5, False), (0, 4, True), (0, 4, False), (0, 4, False), (1, 4, False), (1, 3, True), (1, 3, False), (1, 3, False))
EDGE = (0, 4)
PLANE = [c * COMP + 4 * i for c in range(3) for i in range(24)] + [c * COMP + 120 for c in range(3)]
PLANE_ROWS = 80


def lobatto():
    points = np.array([-1.0, -np.sqrt(3.0 / 7.0), 0.0, np.sqrt(3.0 / 7.0), 1.0])
    weights = np.array([0.1, 49.0 / 90.0, 32.0 / 45.0, 49.0 / 90.0, 0.1])
    factor = np.array(
        [np.prod([points[i] - points[k] for k in range(5) if k != i]) for i in range(5)]
    )
    matrix = np.zeros((5, 5))
    for i in range(5):
        for j in range(5):
            if i == j:
                matrix[i, j] = sum((1.0 / (points[i] - points[k]) for k in range(5) if k != i))
            else:
                matrix[i, j] = factor[i] / (factor[j] * (points[i] - points[j]))
    return matrix, weights


def point_row(a, b, k):
    if a < 4 and b < 4:
        return (k * 16 if k < 4 else 64) + b * 4 + a
    if a < 4:
        return (80 + k * 4 if k < 4 else 120) + a
    if b < 4:
        return 96 + k * 4 + b if k < 4 else 112 + b
    return 116 + k if k < 4 else 124


def element_matrices():
    matrix, weights = lobatto()
    eye = np.eye(5)
    grads = [
        np.einsum("ai,bj,ck->abcijk", *[matrix if x == y else eye for y in range(3)]).reshape(125, 125)
        for x in range(3)
    ]
    cube = np.einsum("a,b,c->abc", weights, weights, weights).reshape(125)
    order = np.array([point_row(a, b, k) for a in range(5) for b in range(5) for k in range(5)])
    both = np.zeros((FULL, 2 * FULL))
    for c in range(3):
        for d in range(3):
            first = grads[c].T @ (cube[:, None] * grads[d])
            shear = grads[d].T @ (cube[:, None] * grads[c])
            if c == d:
                shear = shear + sum(g.T @ (cube[:, None] * g) for g in grads)
            both[np.ix_(c * COMP + order, d * COMP + order)] = first
            both[np.ix_(c * COMP + order, FULL + d * COMP + order)] = shear
    high = both.astype(np.float32).astype(ml_dtypes.bfloat16)
    low = (both - high.astype(np.float64)).astype(np.float32).astype(ml_dtypes.bfloat16)
    edge = np.zeros((2, PLANE_ROWS, 2 * FULL), high.dtype)
    edge[0, : len(PLANE)], edge[1, : len(PLANE)] = high[PLANE], low[PLANE]
    return np.concatenate([high, low, edge[0], edge[1]], axis=0)


def lanes(x, index):
    return jnp.take_along_axis(x, index, axis=1, mode="promise_in_bounds")


def wide(row):
    return jnp.broadcast_to(row, (SUB, LANE))


def as_column(row):
    n = row.shape[1]
    diag = lax.broadcasted_iota(jnp.int32, (n, n), 0) == lax.broadcasted_iota(jnp.int32, (n, n), 1)
    return jnp.sum(jnp.where(diag, jnp.broadcast_to(row, (n, n)), 0.0), axis=1, keepdims=True)


def pack_kernel(u, v, m, lev, lam, mu, stored, own, out, index, stage, aux, turned, conn):
    n = 64
    turned[:, 0:125] = stored[...].astype(F32)
    conn[...] = turned[...].T.astype(jnp.int32)
    for i in range(16):
        k, b = i // 4, i % 4
        stage[4 * i : 4 * i + 4, 0:64] = conn[pl.ds(5 * b + k, 4, stride=25), :]
    level = lev[...]
    period = jnp.where(level == 0, 8, jnp.where(level == 1, 4, jnp.where(level == 2, 2, 1)))
    last_corner = conn[100:101, :].astype(F32)
    for i, row in enumerate(
        (conn[0:1, :].astype(F32), conn[4:5, :].astype(F32), conn[20:21, :].astype(F32), last_corner,
         lam[...], mu[...], period.astype(F32))
    ):
        aux[i : i + 1, 0:64] = row
    layer = jnp.where(last_corner >= 4096.0, 1.0, 0.0)
    down = lax.broadcasted_iota(jnp.int32, (n, n), 0)
    across = lax.broadcasted_iota(jnp.int32, (n, n), 1)
    number = down.astype(F32)
    same = (as_column(layer) == layer) & (down < across)
    rank = jnp.sum(jnp.where(same, 1.0, 0.0), axis=0, keepdims=True) + 32.0 * layer
    order = jnp.sum(jnp.where(as_column(rank) == across.astype(F32), number, 0.0), axis=0, keepdims=True)
    order = wide(jnp.concatenate([order, order], axis=1).astype(jnp.int32))
    left = lax.broadcasted_iota(jnp.int32, (SUB, LANE), 1) < 64
    order_half = order + jnp.where(left, 0, 64)
    for t in range(4):
        upper, lower = stage[8 * t : 8 * t + 8, :], stage[32 + 8 * t : 40 + 8 * t, :]
        part = jnp.where(left, upper, pltpu.roll(lower, 64, 1))
        index[8 * t : 8 * t + 8, :] = lanes(part, order_half)
        high, low = part >> 7, part & 127
        acc = [jnp.zeros((SUB, LANE), F32) for _ in range(VALUES)]
        for r in range(32):
            here = high == r
            for k in range(VALUES):
                if k < 3:
                    row = u[k : k + 1, r * LANE : (r + 1) * LANE]
                elif k < 6:
                    row = v[k - 3 : k - 2, r * LANE : (r + 1) * LANE]
                else:
                    row = m[r : r + 1, :]
                acc[k] = jnp.where(here, lanes(wide(row), low), acc[k])
        for k in range(VALUES):
            out[k * 32 + 8 * t : k * 32 + 8 * t + 8, :] = lanes(acc[k], order_half)
    out[VALUES * 32 : ROWS, :] = jnp.zeros((16, LANE), F32)
    sorted_aux = lanes(aux[...], order)[:, 0:64]
    corner = {name: sorted_aux[i : i + 1, :] for i, name in enumerate("ozyx")}
    column = {name: as_column(c) for name, c in corner.items()}

    def match(col, row):
        hit = column[col] == corner[row]
        return jnp.sum(jnp.where(hit, number, 0.0), axis=0, keepdims=True)

    slot = jnp.zeros((n, 1), F32)
    for j in range(4):
        count = (lax.broadcasted_iota(jnp.int32, (n, LANE), 1) + (j * LANE + 1)).astype(F32)
        hit = column["o"] == own[j : j + 1, :].astype(F32)
        slot = slot + jnp.sum(jnp.where(hit, count, 0.0), axis=1, keepdims=True)
    slot_row = jnp.sum(jnp.where(down == across, slot, 0.0), axis=0, keepdims=True)
    rows = [
        sorted_aux[4:5, :],
        sorted_aux[5:6, :],
        sorted_aux[6:7, :],
        match("o", "z"),
        match("z", "o"),
        match("o", "y"),
        match("y", "o"),
        match("o", "x"),
        match("x", "o"),
        jnp.where(corner["x"] >= 4096.0, corner["x"] - 4096.0, -1.0),
        jnp.where(slot_row > 0.5, slot_row - 1.0, -2.0),
    ]
    for i, row in enumerate(rows):
        out[VALUES * 32 + i : VALUES * 32 + i + 1, 0:64] = row


def place_kernel(index, place):
    acc = jnp.zeros((64, LANE), F32)
    lane = lax.broadcasted_iota(jnp.int32, (32, LANE), 1).astype(F32)
    sub = lax.broadcasted_iota(jnp.int32, (32, LANE), 0)
    broad = lax.broadcasted_iota(jnp.int32, (LANE, LANE), 0)
    for r in range(32):
        row = index[r : r + 1, :]
        here = sub == (row >> 7)
        left = jnp.concatenate(
            [jnp.where(here, float(r), 0.0), jnp.where(here, lane, 0.0)], axis=0
        ).astype(jnp.bfloat16)
        right = jnp.where(broad == (row & 127), 1.0, 0.0).astype(jnp.bfloat16)
        acc = acc + lax.dot_general(
            left, right, (((1,), (1,)), ((), ())), preferred_element_type=F32
        )
    place[...] = acc.astype(jnp.int32)


def main_kernel(
    flags, own_far, even, odd, r1, r2, r3, s1, s2, s3, place_far, matrix_far, new_u, new_v,
    held, disp, vel, mass, force, high, low, maps, table, own, place, matrix, sems,
):
    parity, me = flags[0], flags[1]
    lane = lax.broadcasted_iota(jnp.int32, (SUB, LANE), 1)
    sub = lax.broadcasted_iota(jnp.int32, (SUB, LANE), 0)
    left, upper = lane < 64, sub < 4
    is_odd = jnp.full((SUB, LANE), parity, jnp.int32) == 1

    def keep(get, position):
        for r in range(0, ROWS, SUB):
            start = position * ROWS + r
            if not isinstance(start, int):
                start = pl.multiple_of(start, SUB)
            held[pl.ds(start, SUB), :] = get(r)

    copies = [
        pltpu.make_async_copy(far, near, sems.at[i])
        for i, (far, near) in enumerate(((own_far, own), (matrix_far, matrix), (place_far, place)))
    ]
    for copy in copies:
        copy.start()
    keep(lambda r: jnp.where(is_odd, even[r : r + SUB, :], odd[r : r + SUB, :]), 0)
    keep(lambda r: jnp.where(is_odd, odd[r : r + SUB, :], even[r : r + SUB, :]), 8)
    keep(lambda r: jnp.zeros((SUB, LANE), F32), 9)
    for other, near, cross in ((1, r1, s1), (2, r2, s2), (3, r3, s3)):
        partner = lax.bitwise_xor(me, other)
        away = partner - me
        keep(lambda r, near=near: near[r : r + SUB, :], 4 + away)
        keep(lambda r, cross=cross: cross[r : r + SUB, :], jnp.where(away > 0, away, away + 8))
    copies[0].wait()
    keep(lambda r: own[r : r + SUB, :], 4)

    step = jnp.float32(substep_length)
    for t in range(TILES):
        for r in range(0, VALUES * 32, SUB):
            x = held[2 * t * ROWS + r : 2 * t * ROWS + r + SUB, :]
            y = held[(2 * t + 1) * ROWS + r : (2 * t + 1) * ROWS + r + SUB, :]
            near = jnp.where(left, x, pltpu.roll(y, 64, 1))
            far = jnp.where(left, pltpu.roll(x, 64, 1), y)
            k, q = r // 32, r % 32
            for p, value in ((q, near), (q + 32, far)):
                if k < 3:
                    row = t * FULL + k * COMP + p
                    disp[row : row + SUB, :] = value
                elif k < 6:
                    row = (t * 3 + k - 3) * 64 + p
                    vel[row : row + SUB, :] = value
                else:
                    row = t * 64 + p
                    mass[row : row + SUB, :] = step * value
        for c in range(3):
            row = t * FULL + c * COMP + 120
            disp[row : row + SUB, :] = jnp.zeros((SUB, LANE), F32)

    def elem(j, i):
        row = j * ROWS + VALUES * 32 + i
        return held[row : row + 1, :]

    ghost = jnp.concatenate([elem(j, 9) for j in range(8)], axis=0)
    corner = jnp.concatenate([elem(j + 1, 10) for j in range(8)], axis=0)
    ghost_t, corner_t = ghost.T, corner.T
    count = lax.broadcasted_iota(jnp.int32, (32, LANE), 0).astype(F32)
    to_next, to_prev = [], []
    for j in range(8):
        hit = corner_t[0:32, j : j + 1] == ghost[j : j + 1, :]
        to_next.append(jnp.sum(jnp.where(hit, count, 0.0), axis=0, keepdims=True))
        hit = ghost_t[32:64, j : j + 1] == corner[j : j + 1, :]
        to_prev.append(jnp.sum(jnp.where(hit, count + 32.0, 0.0), axis=0, keepdims=True))
    none = jnp.zeros((1, LANE), F32)
    to_next += [none, none]
    to_prev = [none] + to_prev + [none]
    half = jnp.where(lane[0:1, :] < 64, 0.0, 64.0)
    first_half = lane[0:1, :] < 64
    layer = (lane[0:1, :] & 63) >= 32

    def join(x, y):
        return jnp.where(first_half, x, pltpu.roll(wide(y), 64, 1)[0:1, :])

    def map_at(t, kind):
        row = (t * 6 + kind) * SUB
        return maps[row : row + SUB, :]

    lame, shear, period = [], [], []
    for t in range(TILES):
        x, y = 2 * t, 2 * t + 1
        lame.append(join(elem(x, 0), elem(y, 0)))
        shear.append(join(elem(x, 1), elem(y, 1)))
        period.append(join(elem(x, 2), elem(y, 2)).astype(jnp.int32))
        rows = [join(elem(x, i), elem(y, i)) + half for i in (3, 4, 5, 6)]
        inside = join(elem(x, 7), elem(y, 7)) + half
        outside = join(to_next[x] + 64.0, to_next[y])
        rows.append(jnp.where(layer, outside, inside))
        inside = join(elem(x, 8), elem(y, 8)) + half
        outside = join(to_prev[x] + 64.0, to_prev[y])
        rows.append(jnp.where(layer, inside, outside))
        for kind, row in enumerate(rows):
            maps[(t * 6 + kind) * SUB : (t * 6 + kind + 1) * SUB, :] = wide(row.astype(jnp.int32))

    def faces(t):
        for c in range(3):
            o = t * FULL + c * COMP
            for r in (0, 8):
                disp[o + 64 + r : o + 72 + r, :] = lanes(disp[o + r : o + r + 8, :], map_at(t, 0))
        for c in range(3):
            o = t * FULL + c * COMP
            for r in (0, 32):
                x = jnp.where(upper, disp[o + r : o + r + 8, :], disp[o + r + 12 : o + r + 20, :])
                to = o + 80 + r // 4
                disp[to : to + 8, :] = lanes(x, map_at(t, 2))
        o = t * FULL
        x = jnp.where(upper, disp[o + 64 : o + 72, :], disp[o + COMP + 60 : o + COMP + 68, :])
        x = lanes(x, map_at(t, 2))
        disp[o + 120 : o + 124, :] = x[0:4, :]
        disp[o + COMP + 120 : o + COMP + 124, :] = x[4:8, :]
        o = o + 2 * COMP
        disp[o + 120 : o + 124, :] = lanes(disp[o + 64 : o + 72, :], map_at(t, 2))[0:4, :]

    def corners(ref, t, row):
        o = t * FULL + row
        x = jnp.where(sub == 1, ref[o + COMP - 1 : o + COMP + 7, :], ref[o + 2 * COMP - 2 : o + 2 * COMP + 6, :])
        return jnp.where(sub == 0, ref[o : o + 8, :], x)

    def ahead(t, following):
        def pick(x, y):
            return lanes(jnp.where(lane < 32, y, x), map_at(t, 4))

        for c in range(3):
            for i in range(3):
                x = disp[pl.ds(t * FULL + c * COMP + 32 * i, SUB, stride=4), :]
                y = disp[pl.ds(following * FULL + c * COMP + 32 * i, SUB, stride=4), :]
                to = t * FULL + c * COMP + 96 + 8 * i
                disp[to : to + 8, :] = pick(x, y)
        x = pick(corners(disp, t, 120), corners(disp, following, 120))
        for c in range(3):
            row = t * FULL + c * COMP + 124
            disp[row : row + 1, :] = x[c : c + 1, :]

    def collect(t, before):
        def pick(x, y):
            return lanes(jnp.where(lane >= 96, y, x), map_at(t, 5))

        for c in range(3):
            for i in range(3):
                row = t * FULL + c * COMP + 96 + 8 * i
                other = before * FULL + c * COMP + 96 + 8 * i
                x = pick(force[row : row + 8, :], force[other : other + 8, :])
                where = pl.ds(t * FULL + c * COMP + 32 * i, SUB, stride=4)
                force[where, :] = force[where, :] + x
        o, w = t * FULL + 120, before * FULL + 120
        mine = jnp.concatenate([force[o + c * COMP + 4 : o + c * COMP + 5, :] for c in range(3)] + [wide(none)[0:5, :]], axis=0)
        theirs = jnp.concatenate([force[w + c * COMP + 4 : w + c * COMP + 5, :] for c in range(3)] + [wide(none)[0:5, :]], axis=0)
        x = pick(mine, theirs)
        for c in range(3):
            row = o + c * COMP
            force[row : row + 1, :] = force[row : row + 1, :] + x[c : c + 1, :]
        for c in range(3):
            o = t * FULL + c * COMP
            for r in (0, 32):
                row = o + 80 + r // 4
                x = lanes(force[row : row + 8, :], map_at(t, 3))
                force[o + r : o + r + 4, :] = force[o + r : o + r + 4, :] + x[0:4, :]
                force[o + r + 16 : o + r + 20, :] = force[o + r + 16 : o + r + 20, :] + x[4:8, :]
            x = lanes(force[o + 120 : o + 128, :], map_at(t, 3))
            force[o + 64 : o + 68, :] = force[o + 64 : o + 68, :] + x[0:4, :]
        for c in range(3):
            o = t * FULL + c * COMP
            for r in range(0, 64, SUB):
                f = force[o + r : o + r + 8, :]
                if r < 16:
                    f = f + lanes(force[o + 64 + r : o + 72 + r, :], map_at(t, 1))
                row = (t * 3 + c) * 64 + r
                speed = vel[row : row + 8, :] - mass[t * 64 + r : t * 64 + r + 8, :] * f
                vel[row : row + 8, :] = speed
                disp[o + r : o + r + 8, :] = disp[o + r : o + r + 8, :] + step * speed

    copies[1].wait()
    for s, (begin, end, extra) in enumerate(WINDOW):
        for t in range(begin, end + (1 if extra else 0)):
            faces(t)
        groups = [(g, min(g + 2, end)) for g in range(begin, end, 2)]
        for first, last_tile in groups:
            for t in range(first, last_tile):
                ahead(t, t + 1 if t + 1 < end or extra else t)
                weight = jnp.where((s & (period[t] - 1)) == 0, period[t], 0).astype(F32)
                u = disp[t * FULL : (t + 1) * FULL, :]
                for i, factor in enumerate((lame[t] * weight, shear[t] * weight)):
                    x = u * factor
                    head = x.astype(BF16)
                    high[i * FULL : (i + 1) * FULL, t * LANE : (t + 1) * LANE] = head
                    low[i * FULL : (i + 1) * FULL, t * LANE : (t + 1) * LANE] = (x - head.astype(F32)).astype(BF16)
            span = slice(first * LANE, last_tile * LANE)
            if s in EDGE and last_tile == end:
                t = first
                edge = matrix[2 * FULL : 2 * FULL + 2 * PLANE_ROWS, :]
                both = jnp.dot(edge, high[:, span], preferred_element_type=F32)
                total = both[0:PLANE_ROWS] + both[PLANE_ROWS:]
                total = total + jnp.dot(edge[0:PLANE_ROWS], low[:, span], preferred_element_type=F32)
                for r in range(0, FULL, SUB):
                    force[t * FULL + r : t * FULL + r + SUB, :] = jnp.zeros((SUB, LANE), F32)
                for c in range(3):
                    for i in range(3):
                        r = c * 24 + 8 * i
                        force[pl.ds(t * FULL + c * COMP + 32 * i, SUB, stride=4), :] = total[r : r + 8]
                    row = t * FULL + c * COMP + 120
                    force[row : row + 1, :] = total[72 + c : 73 + c]
                continue
            both = jnp.dot(matrix[0 : 2 * FULL, :], high[:, span], preferred_element_type=F32)
            total = both[0:FULL] + both[FULL:] + jnp.dot(matrix[0:FULL, :], low[:, span], preferred_element_type=F32)
            for t in range(first, last_tile):
                force[t * FULL : (t + 1) * FULL, :] = total[:, (t - first) * LANE : (t - first + 1) * LANE]
        for t in range(begin, end):
            collect(t, t - 1 if t > begin else t)

    for c in range(3):
        for q in range(0, 32, SUB):
            row = 2 * FULL + c * COMP + q
            x, y = disp[row : row + 8, :], disp[row + 32 : row + 40, :]
            table[c * 32 + q : c * 32 + q + 8, :] = jnp.where(left, x, pltpu.roll(y, 64, 1))
            row = (6 + c) * 64 + q
            x, y = vel[row : row + 8, :], vel[row + 32 : row + 40, :]
            table[(3 + c) * 32 + q : (3 + c) * 32 + q + 8, :] = jnp.where(left, x, pltpu.roll(y, 64, 1))
    copies[2].wait()
    for t in range(4):
        row, column = place[8 * t : 8 * t + 8, :], place[32 + 8 * t : 32 + 8 * t + 8, :]
        acc = [jnp.zeros((SUB, LANE), F32) for _ in range(6)]
        for q in range(32):
            here = row == q
            for k in range(6):
                value = lanes(wide(table[k * 32 + q : k * 32 + q + 1, :]), column)
                acc[k] = jnp.where(here, value, acc[k])
        for k in range(6):
            for j in range(SUB):
                n = (8 * t + j) * LANE
                ref = new_u if k < 3 else new_v
                ref[k % 3 : k % 3 + 1, n : n + LANE] = acc[k][j : j + 1, :]


VMEM = pl.BlockSpec(memory_space=pltpu.VMEM)
SMEM = pl.BlockSpec(memory_space=pltpu.SMEM)
FAR = pl.BlockSpec(memory_space=pltpu.HBM)


def main_call():
    return pl.pallas_call(
        main_kernel,
        out_shape=(
            jax.ShapeDtypeStruct((3, 4096), F32),
            jax.ShapeDtypeStruct((3, 4096), F32),
        ),
        in_specs=[SMEM, FAR] + [VMEM] * 8 + [FAR, FAR],
        out_specs=(VMEM, VMEM),
        scratch_shapes=[
            pltpu.VMEM((10 * ROWS, LANE), F32),
            pltpu.VMEM((TILES * FULL, LANE), F32),
            pltpu.VMEM((TILES * 3 * 64, LANE), F32),
            pltpu.VMEM((TILES * 64, LANE), F32),
            pltpu.VMEM((TILES * FULL, LANE), F32),
            pltpu.VMEM((2 * FULL, TILES * LANE), BF16),
            pltpu.VMEM((2 * FULL, TILES * LANE), BF16),
            pltpu.VMEM((TILES * 6 * SUB, LANE), jnp.int32),
            pltpu.VMEM((6 * 32, LANE), F32),
            pltpu.VMEM((ROWS, LANE), F32),
            pltpu.VMEM((64, LANE), jnp.int32),
            pltpu.VMEM((2 * FULL + 2 * PLANE_ROWS, 2 * FULL), BF16),
            pltpu.SemaphoreType.DMA((3,)),
        ],
        compiler_params=pltpu.CompilerParams(vmem_limit_bytes=40 * 1024 * 1024),
        name="substeps",
    )


def per_device(displacement, velocity, inverse_mass, levels, first_lame, shear_modulus, connectivity, owner_list):
    rows, across = lax.axis_size("dom"), lax.axis_size("lvl")
    block, index = pl.pallas_call(
        pack_kernel,
        out_shape=(
            jax.ShapeDtypeStruct((ROWS, LANE), F32),
            jax.ShapeDtypeStruct((32, LANE), jnp.int32),
        ),
        in_specs=[VMEM] * 8,
        out_specs=(VMEM, VMEM),
        scratch_shapes=[pltpu.VMEM((64, LANE), jnp.int32), pltpu.VMEM((SUB, LANE), F32),
            pltpu.VMEM((64, LANE), F32), pltpu.VMEM((LANE, 64), jnp.int32)],
        name="pack",
    )(
        displacement,
        velocity,
        inverse_mass.reshape(32, LANE),
        levels.reshape(1, 64),
        first_lame.reshape(1, 64),
        shear_modulus.reshape(1, 64),
        connectivity.T,
        owner_list.reshape(4, LANE),
    )

    def swap_rows(x, shift):
        pairs = []
        for r in range(rows):
            partner = (r ^ 1) if shift == 0 else (((r - 1) ^ 1) + 1) % rows
            pairs += [(r * across + i, partner * across + i) for i in range(across)]
        return lax.ppermute(x, AXES, pairs)

    def swap_near(x, other):
        pairs = [(r * across + i, r * across + (i ^ other)) for r in range(rows) for i in range(across)]
        return lax.ppermute(x, AXES, pairs)

    near = [swap_near(block, other) for other in (1, 2, 3)]
    even = swap_rows(block, 0)
    odd = swap_rows(block, 1)
    matrix = jnp.asarray(element_matrices())
    odd, near[0], even = lax.optimization_barrier((odd, near[0], even))
    place = pl.pallas_call(
        place_kernel,
        out_shape=jax.ShapeDtypeStruct((64, LANE), jnp.int32),
        in_specs=[VMEM],
        out_specs=VMEM,
        name="place",
        cost_estimate=pl.CostEstimate(flops=67_000_000, bytes_accessed=50_000, transcendentals=0),
    )(index)
    parity = lax.axis_index("dom") % 2
    me = lax.axis_index("lvl")
    give_prev_1 = me % 2 == 1
    give_prev_2 = me >= 2
    prev_is_even = parity == 1
    send_1 = jnp.where(give_prev_1 == prev_is_even, even, odd)
    send_2 = jnp.where(give_prev_2 == prev_is_even, even, odd)
    cross = [swap_near(send_1, 1), swap_near(send_2, 2), swap_near(send_2, 3)]
    flags = jnp.stack([parity, me]).astype(jnp.int32)
    hold = lambda x: pltpu.with_memory_space_constraint(x, pltpu.HBM)
    return main_call()(flags, hold(block), even, odd, *near, *cross, hold(place), hold(matrix))


def solution(mesh):
    both = P(None, AXES)
    flat = P(AXES)
    in_specs = (both, both, flat, flat, flat, flat, both, flat)
    return jax.shard_map(
        per_device, mesh=mesh, in_specs=in_specs, out_specs=(both, both), check_vma=False
    )
```

```python
import jax
import jax.numpy as jnp
import ml_dtypes
import numpy as np
from jax import lax
from jax.experimental import pallas as pl
from jax.experimental.pallas import tpu as pltpu
from jax.sharding import PartitionSpec as P

substep_length = 0.01
AXES = ("dom", "lvl")
SUB, LANE = 8, 128
VALUES = 7
ROWS = VALUES * 32 + 16
COMP = 128
FULL = 3 * COMP
TILES = 5
F32, BF16 = jnp.float32, jnp.bfloat16
WINDOW = ((0, 5, False), (0, 4, True), (0, 4, False), (0, 4, False), (1, 4, False), (1, 3, True), (1, 3, False), (1, 3, False))
EDGE = (0, 4)
DONE = (3, 7)
PLANE = [c * COMP + 4 * i for c in range(3) for i in range(24)] + [c * COMP + 120 for c in range(3)]
PLANE_ROWS = 80


def lobatto():
    points = np.array([-1.0, -np.sqrt(3.0 / 7.0), 0.0, np.sqrt(3.0 / 7.0), 1.0])
    weights = np.array([0.1, 49.0 / 90.0, 32.0 / 45.0, 49.0 / 90.0, 0.1])
    factor = np.array(
        [np.prod([points[i] - points[k] for k in range(5) if k != i]) for i in range(5)]
    )
    matrix = np.zeros((5, 5))
    for i in range(5):
        for j in range(5):
            if i == j:
                matrix[i, j] = sum((1.0 / (points[i] - points[k]) for k in range(5) if k != i))
            else:
                matrix[i, j] = factor[i] / (factor[j] * (points[i] - points[j]))
    return matrix, weights


def point_row(a, b, k):
    if a < 4 and b < 4:
        return (k * 16 if k < 4 else 64) + b * 4 + a
    if a < 4:
        return (80 + k * 4 if k < 4 else 120) + a
    if b < 4:
        return 96 + k * 4 + b if k < 4 else 112 + b
    return 116 + k if k < 4 else 124


def element_matrices():
    matrix, weights = lobatto()
    eye = np.eye(5)
    grads = [
        np.einsum("ai,bj,ck->abcijk", *[matrix if x == y else eye for y in range(3)]).reshape(125, 125)
        for x in range(3)
    ]
    cube = np.einsum("a,b,c->abc", weights, weights, weights).reshape(125)
    order = np.array([point_row(a, b, k) for a in range(5) for b in range(5) for k in range(5)])
    both = np.zeros((FULL, 2 * FULL))
    for c in range(3):
        for d in range(3):
            first = grads[c].T @ (cube[:, None] * grads[d])
            shear = grads[d].T @ (cube[:, None] * grads[c])
            if c == d:
                shear = shear + sum(g.T @ (cube[:, None] * g) for g in grads)
            both[np.ix_(c * COMP + order, d * COMP + order)] = first
            both[np.ix_(c * COMP + order, FULL + d * COMP + order)] = shear
    high = both.astype(np.float32).astype(ml_dtypes.bfloat16)
    low = (both - high.astype(np.float64)).astype(np.float32).astype(ml_dtypes.bfloat16)
    edge = np.zeros((2, PLANE_ROWS, 2 * FULL), high.dtype)
    edge[0, : len(PLANE)], edge[1, : len(PLANE)] = high[PLANE], low[PLANE]
    return np.concatenate([high, low, edge[0], edge[1]], axis=0)


def lanes(x, index):
    return jnp.take_along_axis(x, index, axis=1, mode="promise_in_bounds")


def wide(row):
    return jnp.broadcast_to(row, (SUB, LANE))


def as_column(row):
    n = row.shape[1]
    diag = lax.broadcasted_iota(jnp.int32, (n, n), 0) == lax.broadcasted_iota(jnp.int32, (n, n), 1)
    return jnp.sum(jnp.where(diag, jnp.broadcast_to(row, (n, n)), 0.0), axis=1, keepdims=True)


def pack_kernel(u, v, m, lev, lam, mu, stored, own, out, index, stage, aux, turned, conn):
    n = 64
    turned[:, 0:125] = stored[...].astype(F32)
    conn[...] = turned[...].T.astype(jnp.int32)
    for i in range(16):
        k, b = i // 4, i % 4
        stage[4 * i : 4 * i + 4, 0:64] = conn[pl.ds(5 * b + k, 4, stride=25), :]
    level = lev[...]
    period = jnp.where(level == 0, 8, jnp.where(level == 1, 4, jnp.where(level == 2, 2, 1)))
    last_corner = conn[100:101, :].astype(F32)
    for i, row in enumerate(
        (conn[0:1, :].astype(F32), conn[4:5, :].astype(F32), conn[20:21, :].astype(F32), last_corner,
         lam[...], mu[...], period.astype(F32))
    ):
        aux[i : i + 1, 0:64] = row
    layer = jnp.where(last_corner >= 4096.0, 1.0, 0.0)
    down = lax.broadcasted_iota(jnp.int32, (n, n), 0)
    across = lax.broadcasted_iota(jnp.int32, (n, n), 1)
    number = down.astype(F32)
    same = (as_column(layer) == layer) & (down < across)
    rank = jnp.sum(jnp.where(same, 1.0, 0.0), axis=0, keepdims=True) + 32.0 * layer
    order = jnp.sum(jnp.where(as_column(rank) == across.astype(F32), number, 0.0), axis=0, keepdims=True)
    order = wide(jnp.concatenate([order, order], axis=1).astype(jnp.int32))
    left = lax.broadcasted_iota(jnp.int32, (SUB, LANE), 1) < 64
    order_half = order + jnp.where(left, 0, 64)
    for t in range(4):
        upper, lower = stage[8 * t : 8 * t + 8, :], stage[32 + 8 * t : 40 + 8 * t, :]
        part = jnp.where(left, upper, pltpu.roll(lower, 64, 1))
        index[8 * t : 8 * t + 8, :] = lanes(part, order_half)
        high, low = part >> 7, part & 127
        acc = [jnp.zeros((SUB, LANE), F32) for _ in range(VALUES)]
        for r in range(32):
            here = high == r
            for k in range(VALUES):
                if k < 3:
                    row = u[k : k + 1, r * LANE : (r + 1) * LANE]
                elif k < 6:
                    row = v[k - 3 : k - 2, r * LANE : (r + 1) * LANE]
                else:
                    row = m[r : r + 1, :]
                acc[k] = jnp.where(here, lanes(wide(row), low), acc[k])
        for k in range(VALUES):
            out[k * 32 + 8 * t : k * 32 + 8 * t + 8, :] = lanes(acc[k], order_half)
    out[VALUES * 32 : ROWS, :] = jnp.zeros((16, LANE), F32)
    sorted_aux = lanes(aux[...], order)[:, 0:64]
    corner = {name: sorted_aux[i : i + 1, :] for i, name in enumerate("ozyx")}
    column = {name: as_column(c) for name, c in corner.items()}

    def match(col, row):
        hit = column[col] == corner[row]
        return jnp.sum(jnp.where(hit, number, 0.0), axis=0, keepdims=True)

    slot = jnp.zeros((n, 1), F32)
    for j in range(4):
        count = (lax.broadcasted_iota(jnp.int32, (n, LANE), 1) + (j * LANE + 1)).astype(F32)
        hit = column["o"] == own[j : j + 1, :].astype(F32)
        slot = slot + jnp.sum(jnp.where(hit, count, 0.0), axis=1, keepdims=True)
    slot_row = jnp.sum(jnp.where(down == across, slot, 0.0), axis=0, keepdims=True)
    rows = [
        sorted_aux[4:5, :],
        sorted_aux[5:6, :],
        sorted_aux[6:7, :],
        match("o", "z"),
        match("z", "o"),
        match("o", "y"),
        match("y", "o"),
        match("o", "x"),
        match("x", "o"),
        jnp.where(corner["x"] >= 4096.0, corner["x"] - 4096.0, -1.0),
        jnp.where(slot_row > 0.5, slot_row - 1.0, -2.0),
    ]
    for i, row in enumerate(rows):
        out[VALUES * 32 + i : VALUES * 32 + i + 1, 0:64] = row


def place_kernel(index, place):
    acc = jnp.zeros((64, LANE), F32)
    lane = lax.broadcasted_iota(jnp.int32, (32, LANE), 1).astype(F32)
    sub = lax.broadcasted_iota(jnp.int32, (32, LANE), 0)
    broad = lax.broadcasted_iota(jnp.int32, (LANE, LANE), 0)
    for r in range(32):
        row = index[r : r + 1, :]
        here = sub == (row >> 7)
        left = jnp.concatenate(
            [jnp.where(here, float(r), 0.0), jnp.where(here, lane, 0.0)], axis=0
        ).astype(jnp.bfloat16)
        right = jnp.where(broad == (row & 127), 1.0, 0.0).astype(jnp.bfloat16)
        acc = acc + lax.dot_general(
            left, right, (((1,), (1,)), ((), ())), preferred_element_type=F32
        )
    place[...] = acc.astype(jnp.int32)


def main_kernel(
    flags, own_far, even, odd, r1, r2, r3, s1, s2, s3, place_far, matrix_far, new_u, new_v,
    held, disp, vel, mass, force, high, low, maps, table, own, place, matrix, sems,
):
    parity, me = flags[0], flags[1]
    lane = lax.broadcasted_iota(jnp.int32, (SUB, LANE), 1)
    sub = lax.broadcasted_iota(jnp.int32, (SUB, LANE), 0)
    left, upper = lane < 64, sub < 4
    is_odd = jnp.full((SUB, LANE), parity, jnp.int32) == 1

    def keep(get, position):
        for r in range(0, ROWS, SUB):
            start = position * ROWS + r
            if not isinstance(start, int):
                start = pl.multiple_of(start, SUB)
            held[pl.ds(start, SUB), :] = get(r)

    copies = [
        pltpu.make_async_copy(far, near, sems.at[i])
        for i, (far, near) in enumerate(((own_far, own), (matrix_far, matrix), (place_far, place)))
    ]
    for copy in copies:
        copy.start()
    keep(lambda r: jnp.where(is_odd, even[r : r + SUB, :], odd[r : r + SUB, :]), 0)
    keep(lambda r: jnp.where(is_odd, odd[r : r + SUB, :], even[r : r + SUB, :]), 8)
    keep(lambda r: jnp.zeros((SUB, LANE), F32), 9)
    for other, near, cross in ((1, r1, s1), (2, r2, s2), (3, r3, s3)):
        partner = lax.bitwise_xor(me, other)
        away = partner - me
        keep(lambda r, near=near: near[r : r + SUB, :], 4 + away)
        keep(lambda r, cross=cross: cross[r : r + SUB, :], jnp.where(away > 0, away, away + 8))
    copies[0].wait()
    keep(lambda r: own[r : r + SUB, :], 4)

    step = jnp.float32(substep_length)
    for t in range(TILES):
        for r in range(0, VALUES * 32, SUB):
            x = held[2 * t * ROWS + r : 2 * t * ROWS + r + SUB, :]
            y = held[(2 * t + 1) * ROWS + r : (2 * t + 1) * ROWS + r + SUB, :]
            near = jnp.where(left, x, pltpu.roll(y, 64, 1))
            far = jnp.where(left, pltpu.roll(x, 64, 1), y)
            k, q = r // 32, r % 32
            for p, value in ((q, near), (q + 32, far)):
                if k < 3:
                    row = t * FULL + k * COMP + p
                    disp[row : row + SUB, :] = value
                elif k < 6:
                    row = (t * 3 + k - 3) * 64 + p
                    vel[row : row + SUB, :] = value
                else:
                    row = t * 64 + p
                    mass[row : row + SUB, :] = step * value
        for c in range(3):
            row = t * FULL + c * COMP + 120
            disp[row : row + SUB, :] = jnp.zeros((SUB, LANE), F32)

    def elem(j, i):
        row = j * ROWS + VALUES * 32 + i
        return held[row : row + 1, :]

    ghost = jnp.concatenate([elem(j, 9) for j in range(8)], axis=0)
    corner = jnp.concatenate([elem(j + 1, 10) for j in range(8)], axis=0)
    ghost_t, corner_t = ghost.T, corner.T
    count = lax.broadcasted_iota(jnp.int32, (32, LANE), 0).astype(F32)
    to_next, to_prev = [], []
    for j in range(8):
        hit = corner_t[0:32, j : j + 1] == ghost[j : j + 1, :]
        to_next.append(jnp.sum(jnp.where(hit, count, 0.0), axis=0, keepdims=True))
        hit = ghost_t[32:64, j : j + 1] == corner[j : j + 1, :]
        to_prev.append(jnp.sum(jnp.where(hit, count + 32.0, 0.0), axis=0, keepdims=True))
    none = jnp.zeros((1, LANE), F32)
    to_next += [none, none]
    to_prev = [none] + to_prev + [none]
    half = jnp.where(lane[0:1, :] < 64, 0.0, 64.0)
    first_half = lane[0:1, :] < 64
    layer = (lane[0:1, :] & 63) >= 32

    def join(x, y):
        return jnp.where(first_half, x, pltpu.roll(wide(y), 64, 1)[0:1, :])

    def map_at(t, kind):
        row = (t * 6 + kind) * SUB
        return maps[row : row + SUB, :]

    lame, shear, period = [], [], []
    for t in range(TILES):
        x, y = 2 * t, 2 * t + 1
        lame.append(join(elem(x, 0), elem(y, 0)))
        shear.append(join(elem(x, 1), elem(y, 1)))
        period.append(join(elem(x, 2), elem(y, 2)).astype(jnp.int32))
        rows = [join(elem(x, i), elem(y, i)) + half for i in (3, 4, 5, 6)]
        inside = join(elem(x, 7), elem(y, 7)) + half
        outside = join(to_next[x] + 64.0, to_next[y])
        rows.append(jnp.where(layer, outside, inside))
        inside = join(elem(x, 8), elem(y, 8)) + half
        outside = join(to_prev[x] + 64.0, to_prev[y])
        rows.append(jnp.where(layer, inside, outside))
        for kind, row in enumerate(rows):
            maps[(t * 6 + kind) * SUB : (t * 6 + kind + 1) * SUB, :] = wide(row.astype(jnp.int32))

    def faces(t):
        for c in range(3):
            o = t * FULL + c * COMP
            for r in (0, 8):
                disp[o + 64 + r : o + 72 + r, :] = lanes(disp[o + r : o + r + 8, :], map_at(t, 0))
        for c in range(3):
            o = t * FULL + c * COMP
            for r in (0, 32):
                x = jnp.where(upper, disp[o + r : o + r + 8, :], disp[o + r + 12 : o + r + 20, :])
                to = o + 80 + r // 4
                disp[to : to + 8, :] = lanes(x, map_at(t, 2))
        o = t * FULL
        x = jnp.where(upper, disp[o + 64 : o + 72, :], disp[o + COMP + 60 : o + COMP + 68, :])
        x = lanes(x, map_at(t, 2))
        disp[o + 120 : o + 124, :] = x[0:4, :]
        disp[o + COMP + 120 : o + COMP + 124, :] = x[4:8, :]
        o = o + 2 * COMP
        disp[o + 120 : o + 124, :] = lanes(disp[o + 64 : o + 72, :], map_at(t, 2))[0:4, :]

    def corners(ref, t, row):
        o = t * FULL + row
        x = jnp.where(sub == 1, ref[o + COMP - 1 : o + COMP + 7, :], ref[o + 2 * COMP - 2 : o + 2 * COMP + 6, :])
        return jnp.where(sub == 0, ref[o : o + 8, :], x)

    def ahead(t, following):
        def pick(x, y):
            return lanes(jnp.where(lane < 32, y, x), map_at(t, 4))

        for c in range(3):
            for i in range(3):
                x = disp[pl.ds(t * FULL + c * COMP + 32 * i, SUB, stride=4), :]
                y = disp[pl.ds(following * FULL + c * COMP + 32 * i, SUB, stride=4), :]
                to = t * FULL + c * COMP + 96 + 8 * i
                disp[to : to + 8, :] = pick(x, y)
        x = pick(corners(disp, t, 120), corners(disp, following, 120))
        for c in range(3):
            row = t * FULL + c * COMP + 124
            disp[row : row + 1, :] = x[c : c + 1, :]

    def collect(t, before):
        def pick(x, y):
            return lanes(jnp.where(lane >= 96, y, x), map_at(t, 5))

        for c in range(3):
            for i in range(3):
                row = t * FULL + c * COMP + 96 + 8 * i
                other = before * FULL + c * COMP + 96 + 8 * i
                x = pick(force[row : row + 8, :], force[other : other + 8, :])
                where = pl.ds(t * FULL + c * COMP + 32 * i, SUB, stride=4)
                force[where, :] = force[where, :] + x
        o, w = t * FULL + 120, before * FULL + 120
        mine = jnp.concatenate([force[o + c * COMP + 4 : o + c * COMP + 5, :] for c in range(3)] + [wide(none)[0:5, :]], axis=0)
        theirs = jnp.concatenate([force[w + c * COMP + 4 : w + c * COMP + 5, :] for c in range(3)] + [wide(none)[0:5, :]], axis=0)
        x = pick(mine, theirs)
        for c in range(3):
            row = o + c * COMP
            force[row : row + 1, :] = force[row : row + 1, :] + x[c : c + 1, :]
        for c in range(3):
            o = t * FULL + c * COMP
            for r in (0, 32):
                row = o + 80 + r // 4
                x = lanes(force[row : row + 8, :], map_at(t, 3))
                force[o + r : o + r + 4, :] = force[o + r : o + r + 4, :] + x[0:4, :]
                force[o + r + 16 : o + r + 20, :] = force[o + r + 16 : o + r + 20, :] + x[4:8, :]
            x = lanes(force[o + 120 : o + 128, :], map_at(t, 3))
            force[o + 64 : o + 68, :] = force[o + 64 : o + 68, :] + x[0:4, :]
        for c in range(3):
            o = t * FULL + c * COMP
            for r in range(0, 64, SUB):
                f = force[o + r : o + r + 8, :]
                if r < 16:
                    f = f + lanes(force[o + 64 + r : o + 72 + r, :], map_at(t, 1))
                row = (t * 3 + c) * 64 + r
                speed = vel[row : row + 8, :] - mass[t * 64 + r : t * 64 + r + 8, :] * f
                vel[row : row + 8, :] = speed
                disp[o + r : o + r + 8, :] = disp[o + r : o + r + 8, :] + step * speed

    copies[1].wait()
    for s, (begin, end, extra) in enumerate(WINDOW):
        for t in range(begin, end + (1 if extra else 0)):
            faces(t)
        groups = [(g, min(g + 2, end)) for g in range(begin, end, 2)]
        for first, last_tile in groups:
            for t in range(first, last_tile):
                ahead(t, t + 1 if t + 1 < end or extra else t)
                weight = jnp.where((s & (period[t] - 1)) == 0, period[t], 0).astype(F32)
                u = disp[t * FULL : (t + 1) * FULL, :]
                for i, factor in enumerate((lame[t] * weight, shear[t] * weight)):
                    x = u * factor
                    head = x.astype(BF16)
                    high[i * FULL : (i + 1) * FULL, t * LANE : (t + 1) * LANE] = head
                    low[i * FULL : (i + 1) * FULL, t * LANE : (t + 1) * LANE] = (x - head.astype(F32)).astype(BF16)
            span = slice(first * LANE, last_tile * LANE)
            if s in EDGE and last_tile == end:
                t = first
                edge = matrix[2 * FULL : 2 * FULL + 2 * PLANE_ROWS, :]
                both = jnp.dot(edge, high[:, span], preferred_element_type=F32)
                total = both[0:PLANE_ROWS] + both[PLANE_ROWS:]
                total = total + jnp.dot(edge[0:PLANE_ROWS], low[:, span], preferred_element_type=F32)
                for r in range(0, FULL, SUB):
                    force[t * FULL + r : t * FULL + r + SUB, :] = jnp.zeros((SUB, LANE), F32)
                for c in range(3):
                    for i in range(3):
                        r = c * 24 + 8 * i
                        force[pl.ds(t * FULL + c * COMP + 32 * i, SUB, stride=4), :] = total[r : r + 8]
                    row = t * FULL + c * COMP + 120
                    force[row : row + 1, :] = total[72 + c : 73 + c]
                continue
            both = jnp.dot(matrix[0 : 2 * FULL, :], high[:, span], preferred_element_type=F32)
            total = both[0:FULL] + both[FULL:] + jnp.dot(matrix[0:FULL, :], low[:, span], preferred_element_type=F32)
            for t in range(first, last_tile):
                force[t * FULL : (t + 1) * FULL, :] = total[:, (t - first) * LANE : (t - first + 1) * LANE]
        for t in range(begin + (1 if s in DONE else 0), end):
            collect(t, t - 1 if t > begin else t)

    for c in range(3):
        for q in range(0, 32, SUB):
            row = 2 * FULL + c * COMP + q
            x, y = disp[row : row + 8, :], disp[row + 32 : row + 40, :]
            table[c * 32 + q : c * 32 + q + 8, :] = jnp.where(left, x, pltpu.roll(y, 64, 1))
            row = (6 + c) * 64 + q
            x, y = vel[row : row + 8, :], vel[row + 32 : row + 40, :]
            table[(3 + c) * 32 + q : (3 + c) * 32 + q + 8, :] = jnp.where(left, x, pltpu.roll(y, 64, 1))
    copies[2].wait()
    for t in range(4):
        row, column = place[8 * t : 8 * t + 8, :], place[32 + 8 * t : 32 + 8 * t + 8, :]
        acc = [jnp.zeros((SUB, LANE), F32) for _ in range(6)]
        for q in range(32):
            here = row == q
            for k in range(6):
                value = lanes(wide(table[k * 32 + q : k * 32 + q + 1, :]), column)
                acc[k] = jnp.where(here, value, acc[k])
        for k in range(6):
            for j in range(SUB):
                n = (8 * t + j) * LANE
                ref = new_u if k < 3 else new_v
                ref[k % 3 : k % 3 + 1, n : n + LANE] = acc[k][j : j + 1, :]


VMEM = pl.BlockSpec(memory_space=pltpu.VMEM)
SMEM = pl.BlockSpec(memory_space=pltpu.SMEM)
FAR = pl.BlockSpec(memory_space=pltpu.HBM)


def main_call():
    return pl.pallas_call(
        main_kernel,
        out_shape=(
            jax.ShapeDtypeStruct((3, 4096), F32),
            jax.ShapeDtypeStruct((3, 4096), F32),
        ),
        in_specs=[SMEM, FAR] + [VMEM] * 8 + [FAR, FAR],
        out_specs=(VMEM, VMEM),
        scratch_shapes=[
            pltpu.VMEM((10 * ROWS, LANE), F32),
            pltpu.VMEM((TILES * FULL, LANE), F32),
            pltpu.VMEM((TILES * 3 * 64, LANE), F32),
            pltpu.VMEM((TILES * 64, LANE), F32),
            pltpu.VMEM((TILES * FULL, LANE), F32),
            pltpu.VMEM((2 * FULL, TILES * LANE), BF16),
            pltpu.VMEM((2 * FULL, TILES * LANE), BF16),
            pltpu.VMEM((TILES * 6 * SUB, LANE), jnp.int32),
            pltpu.VMEM((6 * 32, LANE), F32),
            pltpu.VMEM((ROWS, LANE), F32),
            pltpu.VMEM((64, LANE), jnp.int32),
            pltpu.VMEM((2 * FULL + 2 * PLANE_ROWS, 2 * FULL), BF16),
            pltpu.SemaphoreType.DMA((3,)),
        ],
        compiler_params=pltpu.CompilerParams(vmem_limit_bytes=40 * 1024 * 1024),
        name="substeps",
    )


def per_device(displacement, velocity, inverse_mass, levels, first_lame, shear_modulus, connectivity, owner_list):
    rows, across = lax.axis_size("dom"), lax.axis_size("lvl")
    block, index = pl.pallas_call(
        pack_kernel,
        out_shape=(
            jax.ShapeDtypeStruct((ROWS, LANE), F32),
            jax.ShapeDtypeStruct((32, LANE), jnp.int32),
        ),
        in_specs=[VMEM] * 8,
        out_specs=(VMEM, VMEM),
        scratch_shapes=[pltpu.VMEM((64, LANE), jnp.int32), pltpu.VMEM((SUB, LANE), F32),
            pltpu.VMEM((64, LANE), F32), pltpu.VMEM((LANE, 64), jnp.int32)],
        name="pack",
    )(
        displacement,
        velocity,
        inverse_mass.reshape(32, LANE),
        levels.reshape(1, 64),
        first_lame.reshape(1, 64),
        shear_modulus.reshape(1, 64),
        connectivity.T,
        owner_list.reshape(4, LANE),
    )

    def swap_rows(x, shift):
        pairs = []
        for r in range(rows):
            partner = (r ^ 1) if shift == 0 else (((r - 1) ^ 1) + 1) % rows
            pairs += [(r * across + i, partner * across + i) for i in range(across)]
        return lax.ppermute(x, AXES, pairs)

    def swap_near(x, other):
        pairs = [(r * across + i, r * across + (i ^ other)) for r in range(rows) for i in range(across)]
        return lax.ppermute(x, AXES, pairs)

    near = [swap_near(block, other) for other in (1, 2, 3)]
    even = swap_rows(block, 0)
    odd = swap_rows(block, 1)
    matrix = jnp.asarray(element_matrices())
    odd, near[0], even = lax.optimization_barrier((odd, near[0], even))
    place = pl.pallas_call(
        place_kernel,
        out_shape=jax.ShapeDtypeStruct((64, LANE), jnp.int32),
        in_specs=[VMEM],
        out_specs=VMEM,
        name="place",
        cost_estimate=pl.CostEstimate(flops=67_000_000, bytes_accessed=50_000, transcendentals=0),
    )(index)
    parity = lax.axis_index("dom") % 2
    me = lax.axis_index("lvl")
    give_prev_1 = me % 2 == 1
    give_prev_2 = me >= 2
    prev_is_even = parity == 1
    send_1 = jnp.where(give_prev_1 == prev_is_even, even, odd)
    send_2 = jnp.where(give_prev_2 == prev_is_even, even, odd)
    cross = [swap_near(send_1, 1), swap_near(send_2, 2), swap_near(send_2, 3)]
    flags = jnp.stack([parity, me]).astype(jnp.int32)
    hold = lambda x: pltpu.with_memory_space_constraint(x, pltpu.HBM)
    return main_call()(flags, hold(block), even, odd, *near, *cross, hold(place), hold(matrix))


def solution(mesh):
    both = P(None, AXES)
    flat = P(AXES)
    in_specs = (both, both, flat, flat, flat, flat, both, flat)
    return jax.shard_map(
        per_device, mesh=mesh, in_specs=in_specs, out_specs=(both, both), check_vma=False
    )
```

```python
import jax
import jax.numpy as jnp
import ml_dtypes
import numpy as np
from jax import lax
from jax.experimental import pallas as pl
from jax.experimental.pallas import tpu as pltpu
from jax.sharding import PartitionSpec as P

substep_length = 0.01
AXES = ("dom", "lvl")
SUB, LANE = 8, 128
VALUES = 7
ROWS = VALUES * 32 + 16
COMP = 128
FULL = 3 * COMP
TILES = 5
F32, BF16 = jnp.float32, jnp.bfloat16
WINDOW = ((0, 5, False), (0, 4, True), (0, 4, False), (0, 4, False), (1, 4, False), (1, 3, True), (1, 3, False), (1, 3, False))
EDGE = (0, 4)
DONE = (3, 7)
PLANE = [c * COMP + 4 * i for c in range(3) for i in range(24)] + [c * COMP + 120 for c in range(3)]
PLANE_ROWS = 80


def lobatto():
    points = np.array([-1.0, -np.sqrt(3.0 / 7.0), 0.0, np.sqrt(3.0 / 7.0), 1.0])
    weights = np.array([0.1, 49.0 / 90.0, 32.0 / 45.0, 49.0 / 90.0, 0.1])
    factor = np.array(
        [np.prod([points[i] - points[k] for k in range(5) if k != i]) for i in range(5)]
    )
    matrix = np.zeros((5, 5))
    for i in range(5):
        for j in range(5):
            if i == j:
                matrix[i, j] = sum((1.0 / (points[i] - points[k]) for k in range(5) if k != i))
            else:
                matrix[i, j] = factor[i] / (factor[j] * (points[i] - points[j]))
    return matrix, weights


def point_row(a, b, k):
    if a < 4 and b < 4:
        return (k * 16 if k < 4 else 64) + b * 4 + a
    if a < 4:
        return (80 + k * 4 if k < 4 else 120) + a
    if b < 4:
        return 96 + k * 4 + b if k < 4 else 112 + b
    return 116 + k if k < 4 else 124


def element_matrices():
    matrix, weights = lobatto()
    eye = np.eye(5)
    grads = [
        np.einsum("ai,bj,ck->abcijk", *[matrix if x == y else eye for y in range(3)]).reshape(125, 125)
        for x in range(3)
    ]
    cube = np.einsum("a,b,c->abc", weights, weights, weights).reshape(125)
    order = np.array([point_row(a, b, k) for a in range(5) for b in range(5) for k in range(5)])
    both = np.zeros((FULL, 2 * FULL))
    for c in range(3):
        for d in range(3):
            first = grads[c].T @ (cube[:, None] * grads[d])
            shear = grads[d].T @ (cube[:, None] * grads[c])
            if c == d:
                shear = shear + sum(g.T @ (cube[:, None] * g) for g in grads)
            both[np.ix_(c * COMP + order, d * COMP + order)] = first
            both[np.ix_(c * COMP + order, FULL + d * COMP + order)] = shear
    high = both.astype(np.float32).astype(ml_dtypes.bfloat16)
    low = (both - high.astype(np.float64)).astype(np.float32).astype(ml_dtypes.bfloat16)
    edge = np.zeros((2, PLANE_ROWS, 2 * FULL), high.dtype)
    edge[0, : len(PLANE)], edge[1, : len(PLANE)] = high[PLANE], low[PLANE]
    return np.concatenate([high, low, edge[0], edge[1]], axis=0)


def lanes(x, index):
    return jnp.take_along_axis(x, index, axis=1, mode="promise_in_bounds")


def wide(row):
    return jnp.broadcast_to(row, (SUB, LANE))


def as_column(row):
    n = row.shape[1]
    diag = lax.broadcasted_iota(jnp.int32, (n, n), 0) == lax.broadcasted_iota(jnp.int32, (n, n), 1)
    return jnp.sum(jnp.where(diag, jnp.broadcast_to(row, (n, n)), 0.0), axis=1, keepdims=True)


def pack_kernel(u, v, m, lev, lam, mu, stored, own, out, index, stage, aux, turned, conn):
    n = 64
    turned[:, 0:125] = stored[...].astype(F32)
    conn[...] = turned[...].T.astype(jnp.int32)
    for i in range(16):
        k, b = i // 4, i % 4
        stage[4 * i : 4 * i + 4, 0:64] = conn[pl.ds(5 * b + k, 4, stride=25), :]
    level = lev[...]
    period = jnp.where(level == 0, 8, jnp.where(level == 1, 4, jnp.where(level == 2, 2, 1)))
    last_corner = conn[100:101, :].astype(F32)
    for i, row in enumerate(
        (conn[0:1, :].astype(F32), conn[4:5, :].astype(F32), conn[20:21, :].astype(F32), last_corner,
         lam[...], mu[...], period.astype(F32))
    ):
        aux[i : i + 1, 0:64] = row
    layer = jnp.where(last_corner >= 4096.0, 1.0, 0.0)
    down = lax.broadcasted_iota(jnp.int32, (n, n), 0)
    across = lax.broadcasted_iota(jnp.int32, (n, n), 1)
    number = down.astype(F32)
    same = (as_column(layer) == layer) & (down < across)
    rank = jnp.sum(jnp.where(same, 1.0, 0.0), axis=0, keepdims=True) + 32.0 * layer
    order = jnp.sum(jnp.where(as_column(rank) == across.astype(F32), number, 0.0), axis=0, keepdims=True)
    order = wide(jnp.concatenate([order, order], axis=1).astype(jnp.int32))
    left = lax.broadcasted_iota(jnp.int32, (SUB, LANE), 1) < 64
    order_half = order + jnp.where(left, 0, 64)
    for t in range(4):
        upper, lower = stage[8 * t : 8 * t + 8, :], stage[32 + 8 * t : 40 + 8 * t, :]
        part = jnp.where(left, upper, pltpu.roll(lower, 64, 1))
        index[8 * t : 8 * t + 8, :] = lanes(part, order_half)
        high, low = part >> 7, part & 127
        acc = [jnp.zeros((SUB, LANE), F32) for _ in range(VALUES)]
        for r in range(32):
            here = high == r
            for k in range(VALUES):
                if k < 3:
                    row = u[k : k + 1, r * LANE : (r + 1) * LANE]
                elif k < 6:
                    row = v[k - 3 : k - 2, r * LANE : (r + 1) * LANE]
                else:
                    row = m[r : r + 1, :]
                acc[k] = jnp.where(here, lanes(wide(row), low), acc[k])
        for k in range(VALUES):
            out[k * 32 + 8 * t : k * 32 + 8 * t + 8, :] = lanes(acc[k], order_half)
    out[VALUES * 32 : ROWS, :] = jnp.zeros((16, LANE), F32)
    sorted_aux = lanes(aux[...], order)[:, 0:64]
    corner = {name: sorted_aux[i : i + 1, :] for i, name in enumerate("ozyx")}
    column = {name: as_column(c) for name, c in corner.items()}

    def match(col, row):
        hit = column[col] == corner[row]
        return jnp.sum(jnp.where(hit, number, 0.0), axis=0, keepdims=True)

    slot = jnp.zeros((n, 1), F32)
    for j in range(4):
        count = (lax.broadcasted_iota(jnp.int32, (n, LANE), 1) + (j * LANE + 1)).astype(F32)
        hit = column["o"] == own[j : j + 1, :].astype(F32)
        slot = slot + jnp.sum(jnp.where(hit, count, 0.0), axis=1, keepdims=True)
    slot_row = jnp.sum(jnp.where(down == across, slot, 0.0), axis=0, keepdims=True)
    rows = [
        sorted_aux[4:5, :],
        sorted_aux[5:6, :],
        sorted_aux[6:7, :],
        match("o", "z"),
        match("z", "o"),
        match("o", "y"),
        match("y", "o"),
        match("o", "x"),
        match("x", "o"),
        jnp.where(corner["x"] >= 4096.0, corner["x"] - 4096.0, -1.0),
        jnp.where(slot_row > 0.5, slot_row - 1.0, -2.0),
    ]
    for i, row in enumerate(rows):
        out[VALUES * 32 + i : VALUES * 32 + i + 1, 0:64] = row


def place_kernel(index, place):
    acc = jnp.zeros((64, LANE), F32)
    lane = lax.broadcasted_iota(jnp.int32, (32, LANE), 1).astype(F32)
    sub = lax.broadcasted_iota(jnp.int32, (32, LANE), 0)
    broad = lax.broadcasted_iota(jnp.int32, (LANE, LANE), 0)
    for r in range(32):
        row = index[r : r + 1, :]
        here = sub == (row >> 7)
        left = jnp.concatenate(
            [jnp.where(here, float(r), 0.0), jnp.where(here, lane, 0.0)], axis=0
        ).astype(jnp.bfloat16)
        right = jnp.where(broad == (row & 127), 1.0, 0.0).astype(jnp.bfloat16)
        acc = acc + lax.dot_general(
            left, right, (((1,), (1,)), ((), ())), preferred_element_type=F32
        )
    place[...] = acc.astype(jnp.int32)


def main_kernel(
    flags, own_far, even, odd, r1, r2, r3, s1, s2, s3, place_far, matrix_far, new_u, new_v,
    held, disp, vel, mass, force, high, low, maps, table, own, place, matrix, sems,
):
    parity, me = flags[0], flags[1]
    lane = lax.broadcasted_iota(jnp.int32, (SUB, LANE), 1)
    sub = lax.broadcasted_iota(jnp.int32, (SUB, LANE), 0)
    left, upper = lane < 64, sub < 4
    is_odd = jnp.full((SUB, LANE), parity, jnp.int32) == 1

    def keep(get, position):
        for r in range(0, ROWS, SUB):
            start = position * ROWS + r
            if not isinstance(start, int):
                start = pl.multiple_of(start, SUB)
            held[pl.ds(start, SUB), :] = get(r)

    copies = [
        pltpu.make_async_copy(far, near, sems.at[i])
        for i, (far, near) in enumerate(((own_far, own), (matrix_far, matrix), (place_far, place)))
    ]
    for copy in copies:
        copy.start()
    keep(lambda r: jnp.where(is_odd, even[r : r + SUB, :], odd[r : r + SUB, :]), 0)
    keep(lambda r: jnp.where(is_odd, odd[r : r + SUB, :], even[r : r + SUB, :]), 8)
    keep(lambda r: jnp.zeros((SUB, LANE), F32), 9)
    for other, near, cross in ((1, r1, s1), (2, r2, s2), (3, r3, s3)):
        partner = lax.bitwise_xor(me, other)
        away = partner - me
        keep(lambda r, near=near: near[r : r + SUB, :], 4 + away)
        keep(lambda r, cross=cross: cross[r : r + SUB, :], jnp.where(away > 0, away, away + 8))
    copies[0].wait()
    keep(lambda r: own[r : r + SUB, :], 4)

    step = jnp.float32(substep_length)
    for t in range(TILES):
        for r in range(0, VALUES * 32, SUB):
            x = held[2 * t * ROWS + r : 2 * t * ROWS + r + SUB, :]
            y = held[(2 * t + 1) * ROWS + r : (2 * t + 1) * ROWS + r + SUB, :]
            near = jnp.where(left, x, pltpu.roll(y, 64, 1))
            far = jnp.where(left, pltpu.roll(x, 64, 1), y)
            k, q = r // 32, r % 32
            for p, value in ((q, near), (q + 32, far)):
                if k < 3:
                    row = t * FULL + k * COMP + p
                    disp[row : row + SUB, :] = value
                elif k < 6:
                    row = (t * 3 + k - 3) * 64 + p
                    vel[row : row + SUB, :] = value
                else:
                    row = t * 64 + p
                    mass[row : row + SUB, :] = step * value
        for c in range(3):
            row = t * FULL + c * COMP + 120
            disp[row : row + SUB, :] = jnp.zeros((SUB, LANE), F32)

    def elem(j, i):
        row = j * ROWS + VALUES * 32 + i
        return held[row : row + 1, :]

    ghost = jnp.concatenate([elem(j, 9) for j in range(8)], axis=0)
    corner = jnp.concatenate([elem(j + 1, 10) for j in range(8)], axis=0)
    ghost_t, corner_t = ghost.T, corner.T
    count = lax.broadcasted_iota(jnp.int32, (32, LANE), 0).astype(F32)
    to_next, to_prev = [], []
    for j in range(8):
        hit = corner_t[0:32, j : j + 1] == ghost[j : j + 1, :]
        to_next.append(jnp.sum(jnp.where(hit, count, 0.0), axis=0, keepdims=True))
        hit = ghost_t[32:64, j : j + 1] == corner[j : j + 1, :]
        to_prev.append(jnp.sum(jnp.where(hit, count + 32.0, 0.0), axis=0, keepdims=True))
    none = jnp.zeros((1, LANE), F32)
    to_next += [none, none]
    to_prev = [none] + to_prev + [none]
    half = jnp.where(lane[0:1, :] < 64, 0.0, 64.0)
    first_half = lane[0:1, :] < 64
    layer = (lane[0:1, :] & 63) >= 32

    def join(x, y):
        return jnp.where(first_half, x, pltpu.roll(wide(y), 64, 1)[0:1, :])

    def map_at(t, kind):
        row = (t * 6 + kind) * SUB
        return maps[row : row + SUB, :]

    lame, shear, period = [], [], []
    for t in range(TILES):
        x, y = 2 * t, 2 * t + 1
        lame.append(join(elem(x, 0), elem(y, 0)))
        shear.append(join(elem(x, 1), elem(y, 1)))
        period.append(join(elem(x, 2), elem(y, 2)).astype(jnp.int32))
        rows = [join(elem(x, i), elem(y, i)) + half for i in (3, 4, 5, 6)]
        inside = join(elem(x, 7), elem(y, 7)) + half
        outside = join(to_next[x] + 64.0, to_next[y])
        rows.append(jnp.where(layer, outside, inside))
        inside = join(elem(x, 8), elem(y, 8)) + half
        outside = join(to_prev[x] + 64.0, to_prev[y])
        rows.append(jnp.where(layer, inside, outside))
        for kind, row in enumerate(rows):
            maps[(t * 6 + kind) * SUB : (t * 6 + kind + 1) * SUB, :] = wide(row.astype(jnp.int32))

    def faces(t):
        for c in range(3):
            o = t * FULL + c * COMP
            for r in (0, 8):
                disp[o + 64 + r : o + 72 + r, :] = lanes(disp[o + r : o + r + 8, :], map_at(t, 0))
        for c in range(3):
            o = t * FULL + c * COMP
            for r in (0, 32):
                x = jnp.where(upper, disp[o + r : o + r + 8, :], disp[o + r + 12 : o + r + 20, :])
                to = o + 80 + r // 4
                disp[to : to + 8, :] = lanes(x, map_at(t, 2))
        o = t * FULL
        x = jnp.where(upper, disp[o + 64 : o + 72, :], disp[o + COMP + 60 : o + COMP + 68, :])
        x = lanes(x, map_at(t, 2))
        disp[o + 120 : o + 124, :] = x[0:4, :]
        disp[o + COMP + 120 : o + COMP + 124, :] = x[4:8, :]
        o = o + 2 * COMP
        disp[o + 120 : o + 124, :] = lanes(disp[o + 64 : o + 72, :], map_at(t, 2))[0:4, :]

    def corners(ref, t, row):
        o = t * FULL + row
        x = jnp.where(sub == 1, ref[o + COMP - 1 : o + COMP + 7, :], ref[o + 2 * COMP - 2 : o + 2 * COMP + 6, :])
        return jnp.where(sub == 0, ref[o : o + 8, :], x)

    def ahead(t, following):
        def pick(x, y):
            return lanes(jnp.where(lane < 32, y, x), map_at(t, 4))

        for c in range(3):
            for i in range(3):
                x = disp[pl.ds(t * FULL + c * COMP + 32 * i, SUB, stride=4), :]
                y = disp[pl.ds(following * FULL + c * COMP + 32 * i, SUB, stride=4), :]
                to = t * FULL + c * COMP + 96 + 8 * i
                disp[to : to + 8, :] = pick(x, y)
        x = pick(corners(disp, t, 120), corners(disp, following, 120))
        for c in range(3):
            row = t * FULL + c * COMP + 124
            disp[row : row + 1, :] = x[c : c + 1, :]

    def collect(t, before):
        def pick(x, y):
            return lanes(jnp.where(lane >= 96, y, x), map_at(t, 5))

        for c in range(3):
            for i in range(3):
                row = t * FULL + c * COMP + 96 + 8 * i
                other = before * FULL + c * COMP + 96 + 8 * i
                x = pick(force[row : row + 8, :], force[other : other + 8, :])
                where = pl.ds(t * FULL + c * COMP + 32 * i, SUB, stride=4)
                force[where, :] = force[where, :] + x
        o, w = t * FULL + 120, before * FULL + 120
        mine = jnp.concatenate([force[o + c * COMP + 4 : o + c * COMP + 5, :] for c in range(3)] + [wide(none)[0:5, :]], axis=0)
        theirs = jnp.concatenate([force[w + c * COMP + 4 : w + c * COMP + 5, :] for c in range(3)] + [wide(none)[0:5, :]], axis=0)
        x = pick(mine, theirs)
        for c in range(3):
            row = o + c * COMP
            force[row : row + 1, :] = force[row : row + 1, :] + x[c : c + 1, :]
        for c in range(3):
            o = t * FULL + c * COMP
            for r in (0, 32):
                row = o + 80 + r // 4
                x = lanes(force[row : row + 8, :], map_at(t, 3))
                force[o + r : o + r + 4, :] = force[o + r : o + r + 4, :] + x[0:4, :]
                force[o + r + 16 : o + r + 20, :] = force[o + r + 16 : o + r + 20, :] + x[4:8, :]
            x = lanes(force[o + 120 : o + 128, :], map_at(t, 3))
            force[o + 64 : o + 68, :] = force[o + 64 : o + 68, :] + x[0:4, :]
        for c in range(3):
            o = t * FULL + c * COMP
            for r in range(0, 64, SUB):
                f = force[o + r : o + r + 8, :]
                if r < 16:
                    f = f + lanes(force[o + 64 + r : o + 72 + r, :], map_at(t, 1))
                row = (t * 3 + c) * 64 + r
                speed = vel[row : row + 8, :] - mass[t * 64 + r : t * 64 + r + 8, :] * f
                vel[row : row + 8, :] = speed
                disp[o + r : o + r + 8, :] = disp[o + r : o + r + 8, :] + step * speed

    copies[1].wait()
    for s, (begin, end, extra) in enumerate(WINDOW):
        for t in range(begin, end + (1 if extra else 0)):
            faces(t)
        groups = [(g, min(g + 2, end)) for g in range(begin, end, 2)]
        for first, last_tile in groups:
            for t in range(first, last_tile):
                ahead(t, t + 1 if t + 1 < end or extra else t)
                weight = jnp.where((s & (period[t] - 1)) == 0, period[t], 0).astype(F32)
                u = disp[t * FULL : (t + 1) * FULL, :]
                for i, factor in enumerate((lame[t] * weight, shear[t] * weight)):
                    x = u * factor
                    head = x.astype(BF16)
                    high[i * FULL : (i + 1) * FULL, t * LANE : (t + 1) * LANE] = head
                    low[i * FULL : (i + 1) * FULL, t * LANE : (t + 1) * LANE] = (x - head.astype(F32)).astype(BF16)
            span = slice(first * LANE, last_tile * LANE)
            if s in EDGE and last_tile == end:
                t = first
                edge = matrix[2 * FULL : 2 * FULL + 2 * PLANE_ROWS, :]
                both = jnp.dot(edge, high[:, span], preferred_element_type=F32)
                total = both[0:PLANE_ROWS] + both[PLANE_ROWS:]
                total = total + jnp.dot(edge[0:PLANE_ROWS], low[:, span], preferred_element_type=F32)
                for r in range(0, FULL, SUB):
                    force[t * FULL + r : t * FULL + r + SUB, :] = jnp.zeros((SUB, LANE), F32)
                for c in range(3):
                    for i in range(3):
                        r = c * 24 + 8 * i
                        force[pl.ds(t * FULL + c * COMP + 32 * i, SUB, stride=4), :] = total[r : r + 8]
                    row = t * FULL + c * COMP + 120
                    force[row : row + 1, :] = total[72 + c : 73 + c]
                continue
            both = jnp.dot(matrix[0 : 2 * FULL, :], high[:, span], preferred_element_type=F32)
            total = both[0:FULL] + both[FULL:] + jnp.dot(matrix[0:FULL, :], low[:, span], preferred_element_type=F32)
            for t in range(first, last_tile):
                force[t * FULL : (t + 1) * FULL, :] = total[:, (t - first) * LANE : (t - first + 1) * LANE]
        for t in range(begin + (1 if s in DONE else 0), end):
            collect(t, t - 1 if t > begin else t)

    for c in range(3):
        for q in range(0, 32, SUB):
            row = 2 * FULL + c * COMP + q
            x, y = disp[row : row + 8, :], disp[row + 32 : row + 40, :]
            table[c * 32 + q : c * 32 + q + 8, :] = jnp.where(left, x, pltpu.roll(y, 64, 1))
            row = (6 + c) * 64 + q
            x, y = vel[row : row + 8, :], vel[row + 32 : row + 40, :]
            table[(3 + c) * 32 + q : (3 + c) * 32 + q + 8, :] = jnp.where(left, x, pltpu.roll(y, 64, 1))
    copies[2].wait()
    for t in range(4):
        row, column = place[8 * t : 8 * t + 8, :], place[32 + 8 * t : 32 + 8 * t + 8, :]
        acc = [jnp.zeros((SUB, LANE), F32) for _ in range(6)]
        for q in range(32):
            here = row == q
            for k in range(6):
                value = lanes(wide(table[k * 32 + q : k * 32 + q + 1, :]), column)
                acc[k] = jnp.where(here, value, acc[k])
        for k in range(6):
            for j in range(SUB):
                n = (8 * t + j) * LANE
                ref = new_u if k < 3 else new_v
                ref[k % 3 : k % 3 + 1, n : n + LANE] = acc[k][j : j + 1, :]


VMEM = pl.BlockSpec(memory_space=pltpu.VMEM)
SMEM = pl.BlockSpec(memory_space=pltpu.SMEM)
FAR = pl.BlockSpec(memory_space=pltpu.HBM)


def main_call():
    return pl.pallas_call(
        main_kernel,
        out_shape=(
            jax.ShapeDtypeStruct((3, 4096), F32),
            jax.ShapeDtypeStruct((3, 4096), F32),
        ),
        in_specs=[SMEM, FAR] + [VMEM] * 8 + [FAR, FAR],
        out_specs=(VMEM, VMEM),
        scratch_shapes=[
            pltpu.VMEM((10 * ROWS, LANE), F32),
            pltpu.VMEM((TILES * FULL, LANE), F32),
            pltpu.VMEM((TILES * 3 * 64, LANE), F32),
            pltpu.VMEM((TILES * 64, LANE), F32),
            pltpu.VMEM((TILES * FULL, LANE), F32),
            pltpu.VMEM((2 * FULL, TILES * LANE), BF16),
            pltpu.VMEM((2 * FULL, TILES * LANE), BF16),
            pltpu.VMEM((TILES * 6 * SUB, LANE), jnp.int32),
            pltpu.VMEM((6 * 32, LANE), F32),
            pltpu.VMEM((ROWS, LANE), F32),
            pltpu.VMEM((64, LANE), jnp.int32),
            pltpu.VMEM((2 * FULL + 2 * PLANE_ROWS, 2 * FULL), BF16),
            pltpu.SemaphoreType.DMA((3,)),
        ],
        compiler_params=pltpu.CompilerParams(vmem_limit_bytes=40 * 1024 * 1024),
        name="substeps",
    )


def per_device(displacement, velocity, inverse_mass, levels, first_lame, shear_modulus, connectivity, owner_list):
    rows, across = lax.axis_size("dom"), lax.axis_size("lvl")
    block, index = pl.pallas_call(
        pack_kernel,
        out_shape=(
            jax.ShapeDtypeStruct((ROWS, LANE), F32),
            jax.ShapeDtypeStruct((32, LANE), jnp.int32),
        ),
        in_specs=[VMEM] * 8,
        out_specs=(VMEM, VMEM),
        scratch_shapes=[pltpu.VMEM((64, LANE), jnp.int32), pltpu.VMEM((SUB, LANE), F32),
            pltpu.VMEM((64, LANE), F32), pltpu.VMEM((LANE, 64), jnp.int32)],
        name="pack",
    )(
        displacement,
        velocity,
        inverse_mass.reshape(32, LANE),
        levels.reshape(1, 64),
        first_lame.reshape(1, 64),
        shear_modulus.reshape(1, 64),
        connectivity.T,
        owner_list.reshape(4, LANE),
    )

    def swap_rows(x, shift):
        pairs = []
        for r in range(rows):
            partner = (r ^ 1) if shift == 0 else (((r - 1) ^ 1) + 1) % rows
            pairs += [(r * across + i, partner * across + i) for i in range(across)]
        return lax.ppermute(x, AXES, pairs)

    def swap_near(x, other):
        pairs = [(r * across + i, r * across + (i ^ other)) for r in range(rows) for i in range(across)]
        return lax.ppermute(x, AXES, pairs)

    near = [swap_near(block, other) for other in (1, 2, 3)]
    even = swap_rows(block, 0)
    odd = swap_rows(block, 1)
    matrix = jnp.asarray(element_matrices())
    odd, near[0], even = lax.optimization_barrier((odd, near[0], even))
    place = pl.pallas_call(
        place_kernel,
        out_shape=jax.ShapeDtypeStruct((64, LANE), jnp.int32),
        in_specs=[VMEM],
        out_specs=VMEM,
        name="place",
        cost_estimate=pl.CostEstimate(flops=67_000_000, bytes_accessed=50_000, transcendentals=0),
    )(index)
    parity = lax.axis_index("dom") % 2
    me = lax.axis_index("lvl")
    give_prev_1 = me % 2 == 1
    give_prev_2 = me >= 2
    prev_is_even = parity == 1
    send_1 = jnp.where(give_prev_1 == prev_is_even, even, odd)
    send_2 = jnp.where(give_prev_2 == prev_is_even, even, odd)
    cross = [swap_near(send_1, 1), swap_near(send_2, 2), swap_near(send_2, 3)]
    near[2], near[1], cross[0], cross[2], cross[1] = lax.optimization_barrier((near[2], near[1], cross[0], cross[2], cross[1]))
    flags = jnp.stack([parity, me]).astype(jnp.int32)
    hold = lambda x: pltpu.with_memory_space_constraint(x, pltpu.HBM)
    return main_call()(flags, hold(block), even, odd, *near, *cross, hold(place), hold(matrix))


def solution(mesh):
    both = P(None, AXES)
    flat = P(AXES)
    in_specs = (both, both, flat, flat, flat, flat, both, flat)
    return jax.shard_map(
        per_device, mesh=mesh, in_specs=in_specs, out_specs=(both, both), check_vma=False
    )
```
